32 devices in a mesh: tm: 8 (over y, x, core), floor: 4 (over z).
Axes of the slice: x: 2, y: 2, z: 4, core: 2. Of those that a mesh axis runs over, the one named last changes fastest.
Arguments:
- samples: bfloat16 [8, 16, 32768], P('tm', None, 'floor'), may hold values from -6 to 6
- operator: bfloat16 [8, 512, 32768], P('tm', None, 'floor'), may hold values from -0.01171875 to 0.01171875
Outputs:
- sensor_data: bfloat16 [8, 16, 512], P('tm', None, 'floor')
The draws below stay inside these ranges and needn't reach their ends.
All inputs are finite; a program needn't handle non-finite values.
Results may differ from the reference program's by a relative error of at most 0.0013.
Values may be sent and summed in bfloat16 or wider, within the bound.
A program may use at most 64 MiB of HBM per device.

```python
import jax
import jax.numpy as jnp
from jax import lax

S = 512
P_SIZE = 32768
K = 16
NT = 8


def level_of(key, shape, cuts, low, high):
    def one(dim, parts):
        heights = jax.random.uniform(jax.random.fold_in(jax.random.fold_in(key, 6), dim), (parts,), jnp.float32, low / len(cuts), high / len(cuts))
        return jnp.repeat(jnp.exp(heights), shape[dim] // parts).reshape((-1,) + (1,) * (len(shape) - dim - 1))

    factor_of = one(*cuts[0])
    for cut in cuts[1:]:
        factor_of = factor_of * one(*cut)
    return factor_of


def noise(rng, dims, width, bound, pieces=(), kind=jnp.bfloat16):
    result = jax.random.normal(rng, dims, jnp.float32) * width
    if len(pieces) > 0:
        result = level_of(rng, dims, pieces, -0.22, 0.18) * result
    return jnp.clip(result, min=-bound, max=bound).astype(kind)


def setup_inputs(seed: int = 0) -> dict:
    splits = jax.random.split(jax.random.key(seed), 3)
    return {
        "samples": noise(splits[0], (NT, K, P_SIZE), 1.0, 6.0, ((0, 8), (2, 4))),
        "operator": noise(splits[1], (NT, S, P_SIZE), (P_SIZE * NT) ** -0.5, 0.01171875, ((0, 8), (2, 4))),
    }


def reference(samples, operator):
    blocks = samples.astype(jnp.float32)

    def add_lag(total, lag):
        kernel = lax.dynamic_index_in_dim(operator, lag, 0, keepdims=False).astype(jnp.float32)
        images = jnp.einsum('tki,si->tks', blocks, kernel)
        padded = jnp.pad(images, ((NT, 0), (0, 0), (0, 0)))
        shifted = lax.dynamic_slice_in_dim(padded, (NT - lag).astype(jnp.int32), NT, 0)
        return total + shifted, None

    start = jnp.zeros((NT, K, S), jnp.float32)
    total, _ = lax.scan(add_lag, start, jnp.arange(NT, dtype=jnp.int32))
    return total.astype(jnp.bfloat16)
```

```python
import functools

import jax
import jax.numpy as jnp
from jax import lax
from jax.experimental import pallas as pl
from jax.experimental.pallas import tpu as pltpu
from jax.sharding import PartitionSpec as P

MESH = pl.DeviceIdType.MESH
LOOK = 1
AHEAD = 2


def each(low, high, body):
    if high - low <= 4:
        for i in range(low, high):
            body(i)
    else:
        def step(i, carry):
            body(i)
            return carry

        lax.fori_loop(low, high, step, 0)


def grid_of(chips):
    rows = 1
    while rows * rows * 4 <= chips and chips % (rows * 2) == 0:
        rows *= 2
    return rows, chips // rows


def kernel(
    n, m, chunks, x_hbm, op_hbm, out_ref, x, far, op, acc, part, total, share,
    own_sem, op_sem, out_sem, pair_sem, fwd_sem, relay_sem, in_sem,
    red_out, red_in, floor_out, floor_in,
):
    me, floor = lax.axis_index("tm"), lax.axis_index("floor")
    chips = n // 2
    rows, cols = grid_of(chips)
    chip, core = lax.div(me, 2), lax.rem(me, 2)
    row, col = lax.div(chip, cols), lax.rem(chip, cols)
    pair = 2 * chip + 1 - core
    k, width = x.shape[2], x.shape[3]
    sensors = op.shape[1]
    share_size = sensors // m

    def columns(c):
        return pl.ds(c * width, width)

    own = [pltpu.make_async_copy(x_hbm.at[0, :, columns(c)], x.at[c, me], own_sem.at[c]) for c in range(chunks)]
    weights = [pltpu.make_async_copy(op_hbm.at[0, :, columns(c)], op.at[c], op_sem.at[c]) for c in range(chunks)]
    for c in range(chunks):
        own[c].start()
        weights[c].start()

    barrier = pltpu.get_barrier_semaphore()
    for step in range(1, n):
        pl.semaphore_signal(barrier, inc=1, device_id={"tm": lax.rem(me + step, n)}, device_id_type=MESH)
    for step in range(1, m):
        pl.semaphore_signal(barrier, inc=1, device_id={"floor": lax.rem(floor + step, m)}, device_id_type=MESH)
    pl.semaphore_wait(barrier, n + m - 2)

    def need(block, at_chip):
        return 2 * at_chip + block < n

    many = max(rows, cols)

    def straight(source, at):
        return (lax.div(source, cols) == lax.div(at, cols)) | (lax.rem(source, cols) == lax.rem(at, cols))

    def relayed(odd, source, block, at, step):
        turn = lax.rem(core + odd, 2) == 0
        r, q = lax.div(source, cols), lax.rem(source, cols)
        r_at, q_at = lax.div(at, cols), lax.rem(at, cols)
        r_to, q_to = lax.rem(r + step, rows), lax.rem(q + step, cols)
        down = (r_at == r) & (step < rows) & (turn | ((r_to == 0) & (q == 0)))
        along = (q_at == q) & (step < cols) & (jnp.logical_not(turn) | ((q_to == 0) & (r == 0)))
        target = jnp.where(r_at == r, r_to * cols + q_at, r_at * cols + q_to)
        return (at != 0) & (down | along) & need(block, target), 2 * target + core

    def route(odd, source, block, at):
        passes = at < 0
        for step in range(1, many):
            passes = passes | relayed(odd, source, block, at, step)[0]
        return straight(source, at) & (need(block, at) | passes), passes

    def make_plan(step, odd):
        other = lax.rem(chip + step, chips)
        block = 2 * other + core
        wanted, _ = route(odd, chip, me, other)
        _, passes = route(odd, other, block, chip)
        near = straight(other, chip)
        here = need(block, chip) & near, need(block, chip) & jnp.logical_not(near)
        alone = here[0] & jnp.logical_not(passes)
        onward = [relayed(odd, other, block, chip, s) for s in range(1, many)]
        return other, block, wanted, passes, here, alone, onward

    plans = {}
    if chips <= 5:
        plans = {(step, odd): make_plan(step, odd) for step in range(1, chips) for odd in (0, 1)}

    def plan(step, c):
        return plans[step, c % 2] if plans else make_plan(step, c % 2)

    others = [2 * lax.rem(chip + step, chips) + 1 - core for step in range(chips)] if plans else None
    def other_here(block):
        near = straight(lax.div(block, 2), chip)
        return need(block, chip) & near, need(block, chip) & jnp.logical_not(near)

    others_here = [other_here(block) for block in others] if plans else None
    self_here = need(me, chip)

    busy = need(2 * row * cols, chip) | need(2 * col, chip)

    def send(c, block, target, sem, source=None, into=None):
        return pltpu.make_async_remote_copy(
            src_ref=x.at[c, block] if source is None else source,
            dst_ref=(x if into is None else into).at[c, block],
            send_sem=sem, recv_sem=in_sem.at[c, block], device_id={"tm": target}, device_id_type=MESH,
        )

    def mine(c):
        return x_hbm.at[0, :, columns(c)]

    def sends(c, act):
        def one(step):
            _, block, wanted, *_ = plan(step, c)

            @pl.when(wanted)
            def _():
                act(send(c, me, block, out_sem.at[c, step], mine(c)))

        each(1, chips, one)

        @pl.when(self_here)
        def _():
            act(send(c, me, pair, pair_sem.at[c], mine(c)))

    def relays(c, act, wait):
        def one(step):
            source, block, _, passes, _, _, onward = plan(step, c)

            @pl.when(passes)
            def _():
                if wait:
                    send(c, block, pair, fwd_sem.at[c, source]).wait_recv()
                for s, (wanted, target) in enumerate(onward):
                    @pl.when(wanted)
                    def _(s=s, target=target):
                        act(send(c, block, target, relay_sem.at[c, source, s], None, far))

        each(1, chips, one)

    def forwards(c, act, wait):
        def one(step):
            source, block, _, _, here, alone, _ = plan(step, c)
            if wait:
                @pl.when(alone)
                def _():
                    send(c, block, pair, fwd_sem.at[c, source]).wait_recv()

            @pl.when(here[0])
            def _():
                act(send(c, block, pair, fwd_sem.at[c, source]))

        each(1, chips, one)

    def far_forwards(c, act, wait):
        def one(step):
            source, block, _, _, here, _, _ = plan(step, c)

            @pl.when(here[1])
            def _():
                copy = send(c, block, pair, fwd_sem.at[c, source], far.at[c, block], far)
                if wait:
                    copy.wait_recv()
                act(copy)

        each(1, chips, one)

    def take(c, part_of):
        def one(step):
            block = others[step] if plans else 2 * lax.rem(chip + step, chips) + 1 - core
            here = (others_here[step] if plans else other_here(block))[part_of]

            @pl.when(here)
            def _():
                send(c, block, pair, pair_sem.at[c], None, far if part_of else None).wait_recv()

        each(0, chips, one)

    def start(copy):
        copy.start()

    def wait_send(copy):
        copy.wait_send()


    tile = min(n, max(1, 128 // k))

    def image_of(block_rows, c):
        return lax.dot_general(
            block_rows.reshape(-1, width), op[c], (((1,), (1,)), ((), ())), preferred_element_type=jnp.float32
        ).reshape(-1, k, sensors)

    for c in range(chunks):
        sends(c, start)
    for c in range(min(LOOK, chunks)):
        relays(c, start, True)
    forwards(0, start, True)
    for c in range(chunks):
        if c + LOOK < chunks:
            relays(c + LOOK, start, True)
        if c + 1 < chunks:
            forwards(c + 1, start, True)
        take(c, 0)
        own[c].wait()
        weights[c].wait()

        @pl.when(busy)
        def _(c=c):
            for r in range(n // tile):
                image = image_of(x[c, r * tile:(r + 1) * tile], c)
                if c == 0:
                    acc[r * tile:(r + 1) * tile] = image
                else:
                    acc[r * tile:(r + 1) * tile] += image

    def lag_part(step):
        return pltpu.make_async_remote_copy(
            src_ref=acc.at[step], dst_ref=part.at[me],
            send_sem=red_out.at[step], recv_sem=red_in.at[me],
            device_id={"tm": lax.rem(me + step, n)}, device_id_type=MESH,
        )

    def lag_parts(near, act):
        for step in range(n - 1, 0, -1):
            @pl.when((me + step < n) & (straight(step // 2, chip) == near))
            def _(step=step):
                act(lag_part(step))

    lag_parts(True, start)

    far_forwards(0, start, True)
    for c in range(chunks):
        if c + 1 < chunks:
            far_forwards(c + 1, start, True)
        take(c, 1)

        def far_images(step, c=c):
            r = lax.rem(row + 1 + lax.div(step, max(1, cols - 1)), rows)
            q = lax.rem(col + 1 + lax.rem(step, max(1, cols - 1)), cols)
            source = r * cols + q

            @pl.when(need(2 * source, chip))
            def _():
                image = image_of(far[c, pl.ds(2 * source, 2)], c)
                if c == 0:
                    acc[pl.ds(2 * source, 2)] = image
                else:
                    acc[pl.ds(2 * source, 2)] += image

        each(0, (rows - 1) * (cols - 1), far_images)

    lag_parts(False, start)

    for c in range(chunks):
        sends(c, wait_send)
        relays(c, wait_send, False)
        forwards(c, wait_send, False)
        far_forwards(c, wait_send, False)

    def add_lag(lag, value):
        pltpu.make_async_remote_copy(
            src_ref=acc.at[0], dst_ref=part.at[lag],
            send_sem=red_out.at[0], recv_sem=red_in.at[lag],
            device_id={"tm": pair}, device_id_type=MESH,
        ).wait_recv()
        return value + part[lag]

    value = lax.fori_loop(0, me, add_lag, acc[0])
    for j in range(m):
        total[j] = value[:, j * share_size:(j + 1) * share_size]

    def to_floor(step):
        other = lax.rem(floor + step, m)
        return pltpu.make_async_remote_copy(
            src_ref=total.at[other], dst_ref=share.at[floor],
            send_sem=floor_out.at[step], recv_sem=floor_in.at[floor],
            device_id={"floor": other}, device_id_type=MESH,
        )

    for step in range(m - 1, 0, -1):
        to_floor(step).start()
    result = total[floor]
    for step in range(1, m):
        source = lax.rem(floor + step, m)
        pltpu.make_async_remote_copy(
            src_ref=total.at[source], dst_ref=share.at[source],
            send_sem=floor_out.at[step], recv_sem=floor_in.at[source],
            device_id={"floor": source}, device_id_type=MESH,
        ).wait_recv()
        result = result + share[source]
    out_ref[0] = result.astype(out_ref.dtype)

    lag_parts(True, wait_send)
    lag_parts(False, wait_send)
    for step in range(1, m):
        to_floor(step).wait_send()


def square(
    m, chunks, split, x_hbm, op_hbm, out_ref, x, op, acc, part, total, share,
    own_sem, op_sem, x_sem, y_sem, pair_sem, pass_sem, fwd_sem, in_sem,
    red_out, red_in, floor_out, floor_in, hello,
):
    n = part.shape[0]
    chips = n // 2
    half = chunks // 2
    me, floor = lax.axis_index("tm"), lax.axis_index("floor")
    chip, core = lax.div(me, 2), lax.rem(me, 2)
    row, col = lax.div(chip, 2), lax.rem(chip, 2)
    sources = [chip, 2 * row + 1 - col, 2 * (1 - row) + col, 2 * (1 - row) + 1 - col]
    pair, at_x, at_y = 2 * chip + 1 - core, 2 * sources[1] + core, 2 * sources[2] + core
    k, width = x.shape[2], x.shape[3]
    share_size = op.shape[1] // m
    first = chip == 0

    def columns(c):
        return pl.ds(pl.multiple_of(c * width, width), width)

    def own(c):
        return pltpu.make_async_copy(x_hbm.at[0, :, columns(c)], x.at[c, core], own_sem.at[c])

    def weights(c):
        return pltpu.make_async_copy(op_hbm.at[0, :, columns(c)], op.at[c], op_sem.at[c])

    def order(p):
        paired = lax.rem(p, 2) * half + lax.div(p, 2)
        return jnp.where((chip == 0) | (chip == chips - 1), paired, lax.rem(p + split, chunks))

    for c in range(chunks):
        own(c).start()
        weights(c).start()

    def greet(sem):
        for target in (pair, at_x, at_y):
            pl.semaphore_signal(sem, inc=1, device_id={"tm": target}, device_id_type=MESH)

        @pl.when(floor > 0)
        def _():
            pl.semaphore_signal(sem, inc=1, device_id={"floor": floor - 1}, device_id_type=MESH)

        @pl.when(floor < m - 1)
        def _():
            pl.semaphore_signal(sem, inc=1, device_id={"floor": floor + 1}, device_id_type=MESH)

    greeted = 3 + jnp.where(floor > 0, 1, 0) + jnp.where(floor < m - 1, 1, 0)
    barrier = pltpu.get_barrier_semaphore()
    greet(barrier)
    pl.semaphore_wait(barrier, greeted)

    def need(source, at):
        return source + at < chips

    needs = [need(source, chip) for source in sources]

    def by_x(source, c):
        outer = (source == 0) | (source == chips - 1)
        return (outer & (c < half)) | ((source == 1) & (c < split)) | ((source == 2) & (c >= split))

    def to_x(source, across_x, c):
        return need(source, across_x) | by_x(source, c)

    def to_y(source, across_y, c):
        return need(source, across_y) | jnp.logical_not(by_x(source, c))

    def send(c, slot, target, sem, into, source=None):
        return pltpu.make_async_remote_copy(
            src_ref=x.at[c, slot] if source is None else source,
            dst_ref=x.at[c, into], send_sem=sem, recv_sem=in_sem.at[c, into],
            device_id={"tm": target}, device_id_type=MESH,
        )

    def mine(c):
        return x_hbm.at[0, :, columns(c)]

    def send_x(c, act):
        @pl.when(to_x(chip, sources[1], c))
        def _():
            act(send(c, core, at_x, x_sem.at[c], 2 + core, mine(c)))

    def send_y(c, act):
        @pl.when(to_y(chip, sources[2], c))
        def _():
            act(send(c, core, at_y, y_sem.at[c], 4 + core, mine(c)))

    def send_pair(c, act):
        @pl.when(needs[0])
        def _():
            act(send(c, core, pair, pair_sem.at[c], core, mine(c)))

    def start(copy):
        copy.start()

    def wait_send(copy):
        copy.wait_send()

    def wait_recv(copy):
        copy.wait_recv()

    def forward(c, near, act):
        act(send(c, 2 * near + core, pair, fwd_sem.at[near, c], 2 * near + core))

    def taken_x(c):
        return to_x(sources[1], chip, c)

    def taken_y(c):
        return to_y(sources[2], chip, c)

    def pass_x(c, act):
        @pl.when(by_x(sources[1], c))
        def _():
            act(send(c, 2 + core, at_y, pass_sem.at[0, c], 6 + core))

    def pass_y(c, act):
        @pl.when(jnp.logical_not(by_x(sources[2], c)))
        def _():
            act(send(c, 4 + core, at_x, pass_sem.at[1, c], 6 + core))

    late_x, late_y = chip == 1, chip == 2

    def first_half(c, _):
        send_x(c, start)
        send_y(c, start)
        return 0

    def second_half(c, _):
        @pl.when(jnp.logical_not(late_x))
        def _():
            send_x(c, start)

        @pl.when(jnp.logical_not(late_y))
        def _():
            send_y(c, start)

        return 0

    lax.fori_loop(0, half, first_half, 0)
    lax.fori_loop(half, chunks, second_half, 0)

    def all_pairs(c, _):
        send_pair(c, start)
        return 0

    lax.fori_loop(0, chunks, all_pairs, 0)
    greet(hello.at[0])
    acc[...] = jnp.zeros_like(acc)

    steps = 2 * chunks

    def near_step(step):
        return jnp.where(first, (step < half) | (step >= half + chunks), step < chunks)

    def near_chunk(step):
        return jnp.where(first & (step >= half), step - chunks, step)

    def far_chunk(step):
        return order(jnp.where(first, step - half, step - chunks))

    def arrive(step):
        near = near_step(step)

        @pl.when(near)
        def _():
            c = near_chunk(step)
            at = jnp.where(chip == 1, lax.rem(c + half, chunks), c)

            @pl.when(taken_y(at))
            def _():
                send(at, 0, pair, in_sem.at[0, 0], 4 + core).wait_recv()
                pass_y(at, start)

            @pl.when(taken_x(c))
            def _():
                send(c, 0, pair, in_sem.at[0, 0], 2 + core).wait_recv()
                pass_x(c, start)

            @pl.when(needs[1])
            def _():
                forward(c, 1, start)

            @pl.when(needs[2])
            def _():
                forward(at, 2, start)

            @pl.when(c == half - 1)
            def _():
                def late(i, _):
                    @pl.when(late_x)
                    def _():
                        send_x(i, start)

                    @pl.when(late_y)
                    def _():
                        send_y(i, start)

                    return 0

                lax.fori_loop(half, chunks, late, 0)

        @pl.when(jnp.logical_not(near))
        def _():
            c = far_chunk(step)
            send(c, 0, pair, in_sem.at[0, 0], 6 + core).wait_recv()
            forward(c, 3, start)

    def image_of(rows, c):
        return lax.dot_general(
            rows.reshape(-1, width), op[c], (((1,), (1,)), ((), ())), preferred_element_type=jnp.float32
        ).reshape(-1, k, op.shape[1])

    spare = 2 * len(sources)

    def compute(step):
        near = near_step(step)
        other = 1 - core

        def prepare(c):
            own(c).wait()
            weights(c).wait()

            @pl.when(needs[0])
            def _():
                send(c, 0, pair, in_sem.at[0, 0], other).wait_recv()

        @pl.when(near)
        def _():
            c = near_chunk(step)
            held = first & (c >= half)

            @pl.when(jnp.logical_not(held))
            def _():
                prepare(c)

            for at in (1, 2):
                @pl.when(needs[at])
                def _(at=at):
                    send(c, 0, pair, in_sem.at[0, 0], 2 * at + other).wait_recv()

            @pl.when(needs[0] | needs[1] | needs[2])
            def _():
                image = image_of(x[c, 0:6], c)
                slot = jnp.where(held, spare, 0)
                acc[pl.ds(slot, 2)] += image[0:2]
                acc[2:6] += image[2:6]

        @pl.when(jnp.logical_not(near))
        def _():
            c = far_chunk(step)
            held = first & (c >= half)

            @pl.when(held)
            def _():
                prepare(c)

            send(c, 0, pair, in_sem.at[0, 0], 6 + other).wait_recv()
            image = image_of(jnp.concatenate([x[c, 0:2], x[c, 6:8]], axis=0), c)
            slot = jnp.where(held, 0, spare)
            acc[pl.ds(slot, 2)] += image[0:2]
            acc[6:8] += image[2:4]

    def lag_part(slot, act):
        block = 2 * sources[slot // 2] + slot % 2

        @pl.when((block > 0) & (block + me < n))
        def _():
            act(pltpu.make_async_remote_copy(
                src_ref=acc.at[slot], dst_ref=part.at[me],
                send_sem=red_out.at[slot], recv_sem=red_in.at[me],
                device_id={"tm": jnp.minimum(block + me, n - 1)}, device_id_type=MESH,
            ))

    def lag_parts(early, act):
        for at in (3, 1, 2, 0):
            now = {0: early, 3: first == early}.get(at, first != early)
            if at == 0 and not early:
                continue

            @pl.when(now)
            def _(at=at):
                for j in (0, 1):
                    lag_part(2 * at + j, act)

    for step in range(AHEAD):
        arrive(step)
    pl.semaphore_wait(hello.at[0], greeted)
    greet(hello.at[1])
    flush = jnp.where(first, half + chunks - 1, chunks - 1)

    def body(step, _):
        @pl.when(step + AHEAD < steps)
        def _():
            arrive(step + AHEAD)

        compute(step)

        @pl.when(step == flush)
        def _():
            pl.semaphore_wait(hello.at[1], greeted)
            lag_parts(True, start)

        return 0

    lax.fori_loop(0, steps, body, 0)
    lag_parts(False, start)

    def drain(c, _):
        send_x(c, wait_send)
        send_y(c, wait_send)
        send_pair(c, wait_send)

        @pl.when(taken_x(c))
        def _():
            pass_x(c, wait_send)

        @pl.when(taken_y(c))
        def _():
            pass_y(c, wait_send)

        for at in (1, 2, 3):
            @pl.when(needs[at])
            def _(at=at):
                forward(c, at, wait_send)

        return 0

    lax.fori_loop(0, chunks, drain, 0)

    def add_lag(i, value):
        lag = me - 1 - i
        pltpu.make_async_remote_copy(
            src_ref=acc.at[0], dst_ref=part.at[lag],
            send_sem=red_out.at[0], recv_sem=red_in.at[lag],
            device_id={"tm": pair}, device_id_type=MESH,
        ).wait_recv()
        return value + part[lag]

    value = lax.fori_loop(0, me, add_lag, acc[2 * chip])
    for j in range(m):
        total[j] = value[:, j * share_size:(j + 1) * share_size]

    def to_floor(other, act):
        act(pltpu.make_async_remote_copy(
            src_ref=total.at[other], dst_ref=share.at[floor],
            send_sem=floor_out.at[other], recv_sem=floor_in.at[floor],
            device_id={"floor": other}, device_id_type=MESH,
        ))

    def each_floor(act):
        for step in range(m - 1, 0, -1):
            @pl.when(floor + step < m)
            def _(step=step):
                act(floor + step)

            @pl.when(floor - step >= 0)
            def _(step=step):
                act(floor - step)

    each_floor(lambda other: to_floor(other, start))
    result = total[floor]
    for step in range(1, m):
        source = lax.rem(floor + step, m)
        pltpu.make_async_remote_copy(
            src_ref=total.at[source], dst_ref=share.at[source],
            send_sem=floor_out.at[source], recv_sem=floor_in.at[source],
            device_id={"floor": source}, device_id_type=MESH,
        ).wait_recv()
        result = result + share[source]
    out_ref[0] = result.astype(out_ref.dtype)

    lag_parts(True, wait_send)
    lag_parts(False, wait_send)
    each_floor(lambda other: to_floor(other, wait_send))


def square_call(n, m, samples, operator):
    _, k, depth = samples.shape
    sensors = operator.shape[1]
    chunks = 8
    width = depth // chunks
    dma = pltpu.SemaphoreType.DMA
    return pl.pallas_call(
        functools.partial(square, m, chunks, chunks // 4),
        out_shape=pltpu.VMEM((1, k, sensors // m), jnp.bfloat16),
        in_specs=[pl.BlockSpec(memory_space=pl.ANY)] * 2,
        out_specs=pl.BlockSpec(memory_space=pltpu.VMEM),
        scratch_shapes=[
            pltpu.VMEM((chunks, n, k, width), jnp.bfloat16),
            pltpu.VMEM((chunks, sensors, width), jnp.bfloat16),
            pltpu.VMEM((n + 2, k, sensors), jnp.float32),
            pltpu.VMEM((n, k, sensors), jnp.float32),
            pltpu.VMEM((m, k, sensors // m), jnp.float32),
            pltpu.VMEM((m, k, sensors // m), jnp.float32),
            dma((chunks,)), dma((chunks,)), dma((chunks,)), dma((chunks,)), dma((chunks,)),
            dma((2, chunks)), dma((4, chunks)), dma((chunks, n)),
            dma((n,)), dma((n,)), dma((m,)), dma((m,)),
            pltpu.SemaphoreType.REGULAR((2,)),
        ],
        compiler_params=pltpu.CompilerParams(collective_id=0, has_side_effects=True),
    )(samples, operator)


def solution(mesh):
    n, m = mesh.shape["tm"], mesh.shape["floor"]

    def local(samples, operator):
        if grid_of(n // 2) == (2, 2):
            return square_call(n, m, samples, operator)
        _, k, depth = samples.shape
        sensors = operator.shape[1]
        chunks = 4
        width = depth // chunks
        return pl.pallas_call(
            functools.partial(kernel, n, m, chunks),
            out_shape=pltpu.VMEM((1, k, sensors // m), jnp.bfloat16),
            in_specs=[pl.BlockSpec(memory_space=pl.ANY)] * 2,
            out_specs=pl.BlockSpec(memory_space=pltpu.VMEM),
            scratch_shapes=[
                pltpu.VMEM((chunks, n, k, width), jnp.bfloat16),
                pltpu.VMEM((chunks, n, k, width), jnp.bfloat16),
                pltpu.VMEM((chunks, sensors, width), jnp.bfloat16),
                pltpu.VMEM((n, k, sensors), jnp.float32),
                pltpu.VMEM((n, k, sensors), jnp.float32),
                pltpu.VMEM((m, k, sensors // m), jnp.float32),
                pltpu.VMEM((m, k, sensors // m), jnp.float32),
                pltpu.SemaphoreType.DMA((chunks,)),
                pltpu.SemaphoreType.DMA((chunks,)),
                pltpu.SemaphoreType.DMA((chunks, n // 2)),
                pltpu.SemaphoreType.DMA((chunks,)),
                pltpu.SemaphoreType.DMA((chunks, n // 2)),
                pltpu.SemaphoreType.DMA((chunks, n // 2, max(1, max(grid_of(n // 2)) - 1))),
                pltpu.SemaphoreType.DMA((chunks, n)),
                pltpu.SemaphoreType.DMA((n,)),
                pltpu.SemaphoreType.DMA((n,)),
                pltpu.SemaphoreType.DMA((m,)),
                pltpu.SemaphoreType.DMA((m,)),
            ],
            compiler_params=pltpu.CompilerParams(collective_id=0, has_side_effects=True),
        )(samples, operator)

    placed = (P("tm", None, "floor"), P("tm", None, "floor"))
    return jax.shard_map(
        local, mesh=mesh, in_specs=placed, out_specs=P("tm", None, "floor"), check_vma=False
    )
```

```python
import functools

import jax
import jax.numpy as jnp
from jax import lax
from jax.experimental import pallas as pl
from jax.experimental.pallas import tpu as pltpu
from jax.sharding import PartitionSpec as P

MESH = pl.DeviceIdType.MESH
LOOK = 1


def each(low, high, body):
    if high - low <= 4:
        for i in range(low, high):
            body(i)
    else:
        def step(i, carry):
            body(i)
            return carry

        lax.fori_loop(low, high, step, 0)


def grid_of(chips):
    rows = 1
    while rows * rows * 4 <= chips and chips % (rows * 2) == 0:
        rows *= 2
    return rows, chips // rows


def kernel(
    n, m, chunks, x_hbm, op_hbm, out_ref, x, far, op, acc, part, total, share,
    own_sem, op_sem, out_sem, pair_sem, fwd_sem, relay_sem, in_sem,
    red_out, red_in, floor_out, floor_in,
):
    me, floor = lax.axis_index("tm"), lax.axis_index("floor")
    chips = n // 2
    rows, cols = grid_of(chips)
    chip, core = lax.div(me, 2), lax.rem(me, 2)
    row, col = lax.div(chip, cols), lax.rem(chip, cols)
    pair = 2 * chip + 1 - core
    k, width = x.shape[2], x.shape[3]
    sensors = op.shape[1]
    share_size = sensors // m

    def columns(c):
        return pl.ds(c * width, width)

    own = [pltpu.make_async_copy(x_hbm.at[0, :, columns(c)], x.at[c, me], own_sem.at[c]) for c in range(chunks)]
    weights = [pltpu.make_async_copy(op_hbm.at[0, :, columns(c)], op.at[c], op_sem.at[c]) for c in range(chunks)]
    for c in range(chunks):
        own[c].start()
        weights[c].start()

    barrier = pltpu.get_barrier_semaphore()
    for step in range(1, n):
        pl.semaphore_signal(barrier, inc=1, device_id={"tm": lax.rem(me + step, n)}, device_id_type=MESH)
    for step in range(1, m):
        pl.semaphore_signal(barrier, inc=1, device_id={"floor": lax.rem(floor + step, m)}, device_id_type=MESH)
    pl.semaphore_wait(barrier, n + m - 2)

    def need(block, at_chip):
        return 2 * at_chip + block < n

    many = max(rows, cols)

    def straight(source, at):
        return (lax.div(source, cols) == lax.div(at, cols)) | (lax.rem(source, cols) == lax.rem(at, cols))

    def relayed(odd, source, block, at, step):
        turn = lax.rem(core + odd, 2) == 0
        r, q = lax.div(source, cols), lax.rem(source, cols)
        r_at, q_at = lax.div(at, cols), lax.rem(at, cols)
        r_to, q_to = lax.rem(r + step, rows), lax.rem(q + step, cols)
        down = (r_at == r) & (step < rows) & (turn | ((r_to == 0) & (q == 0)))
        along = (q_at == q) & (step < cols) & (jnp.logical_not(turn) | ((q_to == 0) & (r == 0)))
        target = jnp.where(r_at == r, r_to * cols + q_at, r_at * cols + q_to)
        return (at != 0) & (down | along) & need(block, target), 2 * target + core

    def route(odd, source, block, at):
        passes = at < 0
        for step in range(1, many):
            passes = passes | relayed(odd, source, block, at, step)[0]
        return straight(source, at) & (need(block, at) | passes), passes

    def make_plan(step, odd):
        other = lax.rem(chip + step, chips)
        block = 2 * other + core
        wanted, _ = route(odd, chip, me, other)
        _, passes = route(odd, other, block, chip)
        near = straight(other, chip)
        here = need(block, chip) & near, need(block, chip) & jnp.logical_not(near)
        alone = here[0] & jnp.logical_not(passes)
        onward = [relayed(odd, other, block, chip, s) for s in range(1, many)]
        return other, block, wanted, passes, here, alone, onward

    plans = {}
    if chips <= 5:
        plans = {(step, odd): make_plan(step, odd) for step in range(1, chips) for odd in (0, 1)}

    def plan(step, c):
        return plans[step, c % 2] if plans else make_plan(step, c % 2)

    others = [2 * lax.rem(chip + step, chips) + 1 - core for step in range(chips)] if plans else None
    def other_here(block):
        near = straight(lax.div(block, 2), chip)
        return need(block, chip) & near, need(block, chip) & jnp.logical_not(near)

    others_here = [other_here(block) for block in others] if plans else None
    self_here = need(me, chip)

    busy = need(2 * row * cols, chip) | need(2 * col, chip)

    def send(c, block, target, sem, source=None, into=None):
        return pltpu.make_async_remote_copy(
            src_ref=x.at[c, block] if source is None else source,
            dst_ref=(x if into is None else into).at[c, block],
            send_sem=sem, recv_sem=in_sem.at[c, block], device_id={"tm": target}, device_id_type=MESH,
        )

    def mine(c):
        return x_hbm.at[0, :, columns(c)]

    def sends(c, act):
        def one(step):
            _, block, wanted, *_ = plan(step, c)

            @pl.when(wanted)
            def _():
                act(send(c, me, block, out_sem.at[c, step], mine(c)))

        each(1, chips, one)

        @pl.when(self_here)
        def _():
            act(send(c, me, pair, pair_sem.at[c], mine(c)))

    def relays(c, act, wait):
        def one(step):
            source, block, _, passes, _, _, onward = plan(step, c)

            @pl.when(passes)
            def _():
                if wait:
                    send(c, block, pair, fwd_sem.at[c, source]).wait_recv()
                for s, (wanted, target) in enumerate(onward):
                    @pl.when(wanted)
                    def _(s=s, target=target):
                        act(send(c, block, target, relay_sem.at[c, source, s], None, far))

        each(1, chips, one)

    def forwards(c, act, wait):
        def one(step):
            source, block, _, _, here, alone, _ = plan(step, c)
            if wait:
                @pl.when(alone)
                def _():
                    send(c, block, pair, fwd_sem.at[c, source]).wait_recv()

            @pl.when(here[0])
            def _():
                act(send(c, block, pair, fwd_sem.at[c, source]))

        each(1, chips, one)

    def far_forwards(c, act, wait):
        def one(step):
            source, block, _, _, here, _, _ = plan(step, c)

            @pl.when(here[1])
            def _():
                copy = send(c, block, pair, fwd_sem.at[c, source], far.at[c, block], far)
                if wait:
                    copy.wait_recv()
                act(copy)

        each(1, chips, one)

    def take(c, part_of):
        def one(step):
            block = others[step] if plans else 2 * lax.rem(chip + step, chips) + 1 - core
            here = (others_here[step] if plans else other_here(block))[part_of]

            @pl.when(here)
            def _():
                send(c, block, pair, pair_sem.at[c], None, far if part_of else None).wait_recv()

        each(0, chips, one)

    def start(copy):
        copy.start()

    def wait_send(copy):
        copy.wait_send()


    tile = min(n, max(1, 128 // k))

    def image_of(block_rows, c):
        return lax.dot_general(
            block_rows.reshape(-1, width), op[c], (((1,), (1,)), ((), ())), preferred_element_type=jnp.float32
        ).reshape(-1, k, sensors)

    for c in range(chunks):
        sends(c, start)
    for c in range(min(LOOK, chunks)):
        relays(c, start, True)
    forwards(0, start, True)
    for c in range(chunks):
        if c + LOOK < chunks:
            relays(c + LOOK, start, True)
        if c + 1 < chunks:
            forwards(c + 1, start, True)
        take(c, 0)
        own[c].wait()
        weights[c].wait()

        @pl.when(busy)
        def _(c=c):
            for r in range(n // tile):
                image = image_of(x[c, r * tile:(r + 1) * tile], c)
                if c == 0:
                    acc[r * tile:(r + 1) * tile] = image
                else:
                    acc[r * tile:(r + 1) * tile] += image

    def lag_part(step):
        return pltpu.make_async_remote_copy(
            src_ref=acc.at[step], dst_ref=part.at[me],
            send_sem=red_out.at[step], recv_sem=red_in.at[me],
            device_id={"tm": lax.rem(me + step, n)}, device_id_type=MESH,
        )

    def lag_parts(near, act):
        for step in range(n - 1, 0, -1):
            @pl.when((me + step < n) & (straight(step // 2, chip) == near))
            def _(step=step):
                act(lag_part(step))

    lag_parts(True, start)

    far_forwards(0, start, True)
    for c in range(chunks):
        if c + 1 < chunks:
            far_forwards(c + 1, start, True)
        take(c, 1)

        def far_images(step, c=c):
            r = lax.rem(row + 1 + lax.div(step, max(1, cols - 1)), rows)
            q = lax.rem(col + 1 + lax.rem(step, max(1, cols - 1)), cols)
            source = r * cols + q

            @pl.when(need(2 * source, chip))
            def _():
                image = image_of(far[c, pl.ds(2 * source, 2)], c)
                if c == 0:
                    acc[pl.ds(2 * source, 2)] = image
                else:
                    acc[pl.ds(2 * source, 2)] += image

        each(0, (rows - 1) * (cols - 1), far_images)

    lag_parts(False, start)

    for c in range(chunks):
        sends(c, wait_send)
        relays(c, wait_send, False)
        forwards(c, wait_send, False)
        far_forwards(c, wait_send, False)

    def add_lag(lag, value):
        pltpu.make_async_remote_copy(
            src_ref=acc.at[0], dst_ref=part.at[lag],
            send_sem=red_out.at[0], recv_sem=red_in.at[lag],
            device_id={"tm": pair}, device_id_type=MESH,
        ).wait_recv()
        return value + part[lag]

    value = lax.fori_loop(0, me, add_lag, acc[0])
    for j in range(m):
        total[j] = value[:, j * share_size:(j + 1) * share_size]

    def to_floor(step):
        other = lax.rem(floor + step, m)
        return pltpu.make_async_remote_copy(
            src_ref=total.at[other], dst_ref=share.at[floor],
            send_sem=floor_out.at[step], recv_sem=floor_in.at[floor],
            device_id={"floor": other}, device_id_type=MESH,
        )

    for step in range(m - 1, 0, -1):
        to_floor(step).start()
    result = total[floor]
    for step in range(1, m):
        source = lax.rem(floor + step, m)
        pltpu.make_async_remote_copy(
            src_ref=total.at[source], dst_ref=share.at[source],
            send_sem=floor_out.at[step], recv_sem=floor_in.at[source],
            device_id={"floor": source}, device_id_type=MESH,
        ).wait_recv()
        result = result + share[source]
    out_ref[0] = result.astype(out_ref.dtype)

    lag_parts(True, wait_send)
    lag_parts(False, wait_send)
    for step in range(1, m):
        to_floor(step).wait_send()


def square(
    m, chunks, split, x_hbm, op_hbm, out_ref, x, mine, op, acc, sums, part, total, share,
    own_sem, mine_sem, op_sem, swap_out, swap_in, pair_sem, x_sem, y_sem, pass_sem, in_sem,
    red_out, red_in, floor_out, floor_in, hello,
):
    n = part.shape[0]
    chips = n // 2
    me, floor = lax.axis_index("tm"), lax.axis_index("floor")
    chip, core = lax.div(me, 2), lax.rem(me, 2)
    row, col = lax.div(chip, 2), lax.rem(chip, 2)
    sources = [chip, 2 * row + 1 - col, 2 * (1 - row) + col, 2 * (1 - row) + 1 - col]
    other = 1 - core
    pair = 2 * chip + other
    k, width = x.shape[2], x.shape[3]
    sensors = op.shape[2]
    share_size = sensors // m
    inner = (chip == 1) | (chip == 2)

    def columns(half, j):
        return pl.ds(pl.multiple_of((half * chunks + j) * width, width), width)

    def own(j):
        return pltpu.make_async_copy(x_hbm.at[0, :, columns(core, j)], x.at[j, core], own_sem.at[j])

    def staged(half, j):
        return pltpu.make_async_copy(x_hbm.at[0, :, columns(half, j)], mine.at[half, j], mine_sem.at[half, j])

    def weights(j):
        return pltpu.make_async_copy(op_hbm.at[0, :, columns(core, j)], op.at[j, core], op_sem.at[j])

    for j in range(chunks):
        for half in (0, 1):
            staged(half, j).start()
    for j in range(chunks):
        own(j).start()

    def greet(sem):
        for target in (pair, 2 * sources[1], 2 * sources[1] + 1, 2 * sources[2], 2 * sources[2] + 1):
            pl.semaphore_signal(sem, inc=1, device_id={"tm": target}, device_id_type=MESH)

        @pl.when(floor > 0)
        def _():
            pl.semaphore_signal(sem, inc=1, device_id={"floor": floor - 1}, device_id_type=MESH)

        @pl.when(floor < m - 1)
        def _():
            pl.semaphore_signal(sem, inc=1, device_id={"floor": floor + 1}, device_id_type=MESH)

    greeted = 5 + jnp.where(floor > 0, 1, 0) + jnp.where(floor < m - 1, 1, 0)
    barrier = pltpu.get_barrier_semaphore()
    greet(barrier)
    pl.semaphore_wait(barrier, greeted)

    def need(source, at):
        return source + at < chips

    needs = [need(source, chip) for source in sources]

    def by_x(source, parity, j):
        outer = (source == 0) | (source == chips - 1)
        through_first = jnp.where(source == 1, j < split, j >= split)
        return (outer & (parity == j % 2)) | (jnp.logical_not(outer) & through_first)

    def remote(src, dst, out, into, target):
        return pltpu.make_async_remote_copy(
            src_ref=src, dst_ref=dst, send_sem=out, recv_sem=into, device_id={"tm": target}, device_id_type=MESH
        )

    def start(copy):
        copy.start()

    def wait_send(copy):
        copy.wait_send()

    def send_x(j, act):
        @pl.when(needs_at_x | by_x(chip, core, j))
        def _():
            for half in (0, 1):
                act(remote(mine.at[half, j], x.at[j, 2 + core], x_sem.at[half, j], in_sem.at[j, 2 + core], 2 * sources[1] + half))

    def send_y(j, act):
        @pl.when(needs_at_y | jnp.logical_not(by_x(chip, core, j)))
        def _():
            for half in (0, 1):
                act(remote(mine.at[half, j], x.at[j, 4 + core], y_sem.at[half, j], in_sem.at[j, 4 + core], 2 * sources[2] + half))

    needs_at_x, needs_at_y = need(chip, sources[1]), need(chip, sources[2])

    def send_pair(j, act):
        act(remote(mine.at[other, j], x.at[j, core], pair_sem.at[j], in_sem.at[j, core], pair))

    def swap(j, act):
        act(remote(op_hbm.at[0, :, columns(other, j)], op.at[j, core], swap_out.at[j], swap_in.at[j], pair))

    def swapped(j):
        remote(op.at[j, core], op.at[j, other], swap_out.at[j], swap_in.at[j], pair).wait_recv()

    def taken(j, slot):
        remote(x.at[j, slot], x.at[j, slot], pair_sem.at[j], in_sem.at[j, slot], pair).wait_recv()

    def pass_x(j, parity, act):
        act(remote(x.at[j, 2 + parity], x.at[j, 6 + parity], pass_sem.at[0, parity, j], in_sem.at[j, 6 + parity], 2 * sources[2] + core))

    def pass_y(j, parity, act):
        act(remote(x.at[j, 4 + parity], x.at[j, 6 + parity], pass_sem.at[1, parity, j], in_sem.at[j, 6 + parity], 2 * sources[1] + core))

    def from_x(j, here, wait, act):
        for parity in (0, 1):
            onward = by_x(sources[1], parity, j)

            @pl.when(here & (needs[1] | onward))
            def _(parity=parity, onward=onward):
                if wait:
                    taken(j, 2 + parity)

                @pl.when(onward)
                def _():
                    pass_x(j, parity, act)

    def from_y(j, here, wait, act):
        for parity in (0, 1):
            onward = jnp.logical_not(by_x(sources[2], parity, j))

            @pl.when(here & (needs[2] | onward))
            def _(parity=parity, onward=onward):
                if wait:
                    taken(j, 4 + parity)

                @pl.when(onward)
                def _():
                    pass_y(j, parity, act)

    lead = chunks // 2
    for j in range(chunks):
        for half in (0, 1):
            staged(half, j).wait()

        @pl.when((j < lead) | jnp.logical_not(needs_at_x))
        def _(j=j):
            send_x(j, start)

        @pl.when((j < lead) | jnp.logical_not(needs_at_y))
        def _(j=j):
            send_y(j, start)

    for j in range(chunks):
        weights(j).start()
        send_pair(j, start)
        swap(j, start)
    greet(hello.at[0])

    def send_late(j):
        @pl.when(needs_at_x)
        def _():
            send_x(j, start)

        @pl.when(needs_at_y)
        def _():
            send_y(j, start)

    for j in range(chunks):
        from_x(j, jnp.logical_not(needs[1]), True, start)
        from_y(j, jnp.logical_not(needs[2]), True, start)
        if j + lead < chunks:
            @pl.when(inner)
            def _(j=j):
                send_late(j + lead)

    pl.semaphore_wait(hello.at[0], greeted)
    greet(hello.at[1])

    def arrive(j):
        from_x(j, needs[1], True, start)
        from_y(j, needs[2], True, start)
        if j == split - 1:
            @pl.when(jnp.logical_not(inner))
            def _():
                for late in range(lead, chunks):
                    send_late(late)

    def compute(j):
        own(j).wait()
        weights(j).wait()
        taken(j, other)
        swapped(j)
        for parity in (0, 1):
            taken(j, 6 + parity)
        image = lax.dot_general(
            x[j].reshape(-1, width), op[j].reshape(-1, width), (((1,), (1,)), ((), ())),
            preferred_element_type=jnp.float32,
        ).reshape(-1, k, 2 * sensors)
        if j == 0:
            acc[...] = image
        else:
            acc[...] += image

    arrive(0)
    for j in range(chunks):
        if j + 1 < chunks:
            arrive(j + 1)
        compute(j)

    pl.semaphore_wait(hello.at[1], greeted)

    def slot_of(block):
        source = block // 2
        across = jnp.where(col == source % 2, 0, 2) + jnp.where(row == source // 2, 0, 4)
        return across + block % 2

    def record(u, act):
        act(pltpu.make_async_remote_copy(
            src_ref=sums.at[u], dst_ref=part.at[me], send_sem=red_out.at[u], recv_sem=red_in.at[me],
            device_id={"tm": jnp.minimum(2 * chip + u, n - 1)}, device_id_type=MESH,
        ))

    def records(act, add):
        for u in range(n - 1, -1, -1):
            @pl.when(2 * chip + u < n)
            def _(u=u):
                if add:
                    value = acc[slot_of(u), :, :sensors]
                    if u > 0:
                        value = value + acc[slot_of(u - 1), :, sensors:]
                    sums[u] = value
                if u > 1:
                    record(u, act)
                else:
                    @pl.when(core != u)
                    def _():
                        record(u, act)

    records(start, True)

    for j in range(chunks):
        send_x(j, wait_send)
        send_y(j, wait_send)
        send_pair(j, wait_send)
        swap(j, wait_send)
        from_x(j, True, False, wait_send)
        from_y(j, True, False, wait_send)

    def add_part(i, value):
        sender = jnp.where(i == 0, pair, 2 * chip - i)
        pltpu.make_async_remote_copy(
            src_ref=sums.at[0], dst_ref=part.at[sender], send_sem=red_out.at[0], recv_sem=red_in.at[sender],
            device_id={"tm": pair}, device_id_type=MESH,
        ).wait_recv()
        return value + part[sender]

    value = lax.fori_loop(0, 2 * chip + 1, add_part, sums[core])
    for j in range(m):
        total[j] = value[:, j * share_size:(j + 1) * share_size]

    def to_floor(other, act):
        act(pltpu.make_async_remote_copy(
            src_ref=total.at[other], dst_ref=share.at[floor],
            send_sem=floor_out.at[other], recv_sem=floor_in.at[floor],
            device_id={"floor": other}, device_id_type=MESH,
        ))

    def each_floor(act):
        for step in range(m - 1, 0, -1):
            @pl.when(floor + step < m)
            def _(step=step):
                act(floor + step)

            @pl.when(floor - step >= 0)
            def _(step=step):
                act(floor - step)

    each_floor(lambda other: to_floor(other, start))
    result = total[floor]
    for step in range(1, m):
        source = lax.rem(floor + step, m)
        pltpu.make_async_remote_copy(
            src_ref=total.at[source], dst_ref=share.at[source],
            send_sem=floor_out.at[source], recv_sem=floor_in.at[source],
            device_id={"floor": source}, device_id_type=MESH,
        ).wait_recv()
        result = result + share[source]
    out_ref[0] = result.astype(out_ref.dtype)

    records(wait_send, False)
    each_floor(lambda other: to_floor(other, wait_send))


def square_call(n, m, samples, operator):
    _, k, depth = samples.shape
    sensors = operator.shape[1]
    chunks = 4
    width = depth // (2 * chunks)
    dma = pltpu.SemaphoreType.DMA
    return pl.pallas_call(
        functools.partial(square, m, chunks, 1),
        out_shape=pltpu.VMEM((1, k, sensors // m), jnp.bfloat16),
        in_specs=[pl.BlockSpec(memory_space=pl.ANY)] * 2,
        out_specs=pl.BlockSpec(memory_space=pltpu.VMEM),
        scratch_shapes=[
            pltpu.VMEM((chunks, n, k, width), jnp.bfloat16),
            pltpu.VMEM((2, chunks, k, width), jnp.bfloat16),
            pltpu.VMEM((chunks, 2, sensors, width), jnp.bfloat16),
            pltpu.VMEM((n, k, 2 * sensors), jnp.float32),
            pltpu.VMEM((n, k, sensors), jnp.float32),
            pltpu.VMEM((n, k, sensors), jnp.float32),
            pltpu.VMEM((m, k, sensors // m), jnp.float32),
            pltpu.VMEM((m, k, sensors // m), jnp.float32),
            dma((chunks,)), dma((2, chunks)), dma((chunks,)), dma((chunks,)), dma((chunks,)), dma((chunks,)),
            dma((2, chunks)), dma((2, chunks)), dma((2, 2, chunks)), dma((chunks, n)),
            dma((n,)), dma((n,)), dma((m,)), dma((m,)),
            pltpu.SemaphoreType.REGULAR((2,)),
        ],
        compiler_params=pltpu.CompilerParams(collective_id=0, has_side_effects=True),
    )(samples, operator)


def solution(mesh):
    n, m = mesh.shape["tm"], mesh.shape["floor"]

    def local(samples, operator):
        if grid_of(n // 2) == (2, 2):
            return square_call(n, m, samples, operator)
        _, k, depth = samples.shape
        sensors = operator.shape[1]
        chunks = 4
        width = depth // chunks
        return pl.pallas_call(
            functools.partial(kernel, n, m, chunks),
            out_shape=pltpu.VMEM((1, k, sensors // m), jnp.bfloat16),
            in_specs=[pl.BlockSpec(memory_space=pl.ANY)] * 2,
            out_specs=pl.BlockSpec(memory_space=pltpu.VMEM),
            scratch_shapes=[
                pltpu.VMEM((chunks, n, k, width), jnp.bfloat16),
                pltpu.VMEM((chunks, n, k, width), jnp.bfloat16),
                pltpu.VMEM((chunks, sensors, width), jnp.bfloat16),
                pltpu.VMEM((n, k, sensors), jnp.float32),
                pltpu.VMEM((n, k, sensors), jnp.float32),
                pltpu.VMEM((m, k, sensors // m), jnp.float32),
                pltpu.VMEM((m, k, sensors // m), jnp.float32),
                pltpu.SemaphoreType.DMA((chunks,)),
                pltpu.SemaphoreType.DMA((chunks,)),
                pltpu.SemaphoreType.DMA((chunks, n // 2)),
                pltpu.SemaphoreType.DMA((chunks,)),
                pltpu.SemaphoreType.DMA((chunks, n // 2)),
                pltpu.SemaphoreType.DMA((chunks, n // 2, max(1, max(grid_of(n // 2)) - 1))),
                pltpu.SemaphoreType.DMA((chunks, n)),
                pltpu.SemaphoreType.DMA((n,)),
                pltpu.SemaphoreType.DMA((n,)),
                pltpu.SemaphoreType.DMA((m,)),
                pltpu.SemaphoreType.DMA((m,)),
            ],
            compiler_params=pltpu.CompilerParams(collective_id=0, has_side_effects=True),
        )(samples, operator)

    placed = (P("tm", None, "floor"), P("tm", None, "floor"))
    return jax.shard_map(
        local, mesh=mesh, in_specs=placed, out_specs=P("tm", None, "floor"), check_vma=False
    )
```

```python
import functools

import jax
import jax.numpy as jnp
from jax import lax
from jax.experimental import pallas as pl
from jax.experimental.pallas import tpu as pltpu
from jax.sharding import PartitionSpec as P

MESH = pl.DeviceIdType.MESH
LOOK = 1


def each(low, high, body):
    if high - low <= 4:
        for i in range(low, high):
            body(i)
    else:
        def step(i, carry):
            body(i)
            return carry

        lax.fori_loop(low, high, step, 0)


def grid_of(chips):
    rows = 1
    while rows * rows * 4 <= chips and chips % (rows * 2) == 0:
        rows *= 2
    return rows, chips // rows


def kernel(
    n, m, chunks, x_hbm, op_hbm, out_ref, x, far, op, acc, part, total, share,
    own_sem, op_sem, out_sem, pair_sem, fwd_sem, relay_sem, in_sem,
    red_out, red_in, floor_out, floor_in,
):
    me, floor = lax.axis_index("tm"), lax.axis_index("floor")
    chips = n // 2
    rows, cols = grid_of(chips)
    chip, core = lax.div(me, 2), lax.rem(me, 2)
    row, col = lax.div(chip, cols), lax.rem(chip, cols)
    pair = 2 * chip + 1 - core
    k, width = x.shape[2], x.shape[3]
    sensors = op.shape[1]
    share_size = sensors // m

    def columns(c):
        return pl.ds(c * width, width)

    own = [pltpu.make_async_copy(x_hbm.at[0, :, columns(c)], x.at[c, me], own_sem.at[c]) for c in range(chunks)]
    weights = [pltpu.make_async_copy(op_hbm.at[0, :, columns(c)], op.at[c], op_sem.at[c]) for c in range(chunks)]
    for c in range(chunks):
        own[c].start()
        weights[c].start()

    barrier = pltpu.get_barrier_semaphore()
    for step in range(1, n):
        pl.semaphore_signal(barrier, inc=1, device_id={"tm": lax.rem(me + step, n)}, device_id_type=MESH)
    for step in range(1, m):
        pl.semaphore_signal(barrier, inc=1, device_id={"floor": lax.rem(floor + step, m)}, device_id_type=MESH)
    pl.semaphore_wait(barrier, n + m - 2)

    def need(block, at_chip):
        return 2 * at_chip + block < n

    many = max(rows, cols)

    def straight(source, at):
        return (lax.div(source, cols) == lax.div(at, cols)) | (lax.rem(source, cols) == lax.rem(at, cols))

    def relayed(odd, source, block, at, step):
        turn = lax.rem(core + odd, 2) == 0
        r, q = lax.div(source, cols), lax.rem(source, cols)
        r_at, q_at = lax.div(at, cols), lax.rem(at, cols)
        r_to, q_to = lax.rem(r + step, rows), lax.rem(q + step, cols)
        down = (r_at == r) & (step < rows) & (turn | ((r_to == 0) & (q == 0)))
        along = (q_at == q) & (step < cols) & (jnp.logical_not(turn) | ((q_to == 0) & (r == 0)))
        target = jnp.where(r_at == r, r_to * cols + q_at, r_at * cols + q_to)
        return (at != 0) & (down | along) & need(block, target), 2 * target + core

    def route(odd, source, block, at):
        passes = at < 0
        for step in range(1, many):
            passes = passes | relayed(odd, source, block, at, step)[0]
        return straight(source, at) & (need(block, at) | passes), passes

    def make_plan(step, odd):
        other = lax.rem(chip + step, chips)
        block = 2 * other + core
        wanted, _ = route(odd, chip, me, other)
        _, passes = route(odd, other, block, chip)
        near = straight(other, chip)
        here = need(block, chip) & near, need(block, chip) & jnp.logical_not(near)
        alone = here[0] & jnp.logical_not(passes)
        onward = [relayed(odd, other, block, chip, s) for s in range(1, many)]
        return other, block, wanted, passes, here, alone, onward

    plans = {}
    if chips <= 5:
        plans = {(step, odd): make_plan(step, odd) for step in range(1, chips) for odd in (0, 1)}

    def plan(step, c):
        return plans[step, c % 2] if plans else make_plan(step, c % 2)

    others = [2 * lax.rem(chip + step, chips) + 1 - core for step in range(chips)] if plans else None
    def other_here(block):
        near = straight(lax.div(block, 2), chip)
        return need(block, chip) & near, need(block, chip) & jnp.logical_not(near)

    others_here = [other_here(block) for block in others] if plans else None
    self_here = need(me, chip)

    busy = need(2 * row * cols, chip) | need(2 * col, chip)

    def send(c, block, target, sem, source=None, into=None):
        return pltpu.make_async_remote_copy(
            src_ref=x.at[c, block] if source is None else source,
            dst_ref=(x if into is None else into).at[c, block],
            send_sem=sem, recv_sem=in_sem.at[c, block], device_id={"tm": target}, device_id_type=MESH,
        )

    def mine(c):
        return x_hbm.at[0, :, columns(c)]

    def sends(c, act):
        def one(step):
            _, block, wanted, *_ = plan(step, c)

            @pl.when(wanted)
            def _():
                act(send(c, me, block, out_sem.at[c, step], mine(c)))

        each(1, chips, one)

        @pl.when(self_here)
        def _():
            act(send(c, me, pair, pair_sem.at[c], mine(c)))

    def relays(c, act, wait):
        def one(step):
            source, block, _, passes, _, _, onward = plan(step, c)

            @pl.when(passes)
            def _():
                if wait:
                    send(c, block, pair, fwd_sem.at[c, source]).wait_recv()
                for s, (wanted, target) in enumerate(onward):
                    @pl.when(wanted)
                    def _(s=s, target=target):
                        act(send(c, block, target, relay_sem.at[c, source, s], None, far))

        each(1, chips, one)

    def forwards(c, act, wait):
        def one(step):
            source, block, _, _, here, alone, _ = plan(step, c)
            if wait:
                @pl.when(alone)
                def _():
                    send(c, block, pair, fwd_sem.at[c, source]).wait_recv()

            @pl.when(here[0])
            def _():
                act(send(c, block, pair, fwd_sem.at[c, source]))

        each(1, chips, one)

    def far_forwards(c, act, wait):
        def one(step):
            source, block, _, _, here, _, _ = plan(step, c)

            @pl.when(here[1])
            def _():
                copy = send(c, block, pair, fwd_sem.at[c, source], far.at[c, block], far)
                if wait:
                    copy.wait_recv()
                act(copy)

        each(1, chips, one)

    def take(c, part_of):
        def one(step):
            block = others[step] if plans else 2 * lax.rem(chip + step, chips) + 1 - core
            here = (others_here[step] if plans else other_here(block))[part_of]

            @pl.when(here)
            def _():
                send(c, block, pair, pair_sem.at[c], None, far if part_of else None).wait_recv()

        each(0, chips, one)

    def start(copy):
        copy.start()

    def wait_send(copy):
        copy.wait_send()


    tile = min(n, max(1, 128 // k))

    def image_of(block_rows, c):
        return lax.dot_general(
            block_rows.reshape(-1, width), op[c], (((1,), (1,)), ((), ())), preferred_element_type=jnp.float32
        ).reshape(-1, k, sensors)

    for c in range(chunks):
        sends(c, start)
    for c in range(min(LOOK, chunks)):
        relays(c, start, True)
    forwards(0, start, True)
    for c in range(chunks):
        if c + LOOK < chunks:
            relays(c + LOOK, start, True)
        if c + 1 < chunks:
            forwards(c + 1, start, True)
        take(c, 0)
        own[c].wait()
        weights[c].wait()

        @pl.when(busy)
        def _(c=c):
            for r in range(n // tile):
                image = image_of(x[c, r * tile:(r + 1) * tile], c)
                if c == 0:
                    acc[r * tile:(r + 1) * tile] = image
                else:
                    acc[r * tile:(r + 1) * tile] += image

    def lag_part(step):
        return pltpu.make_async_remote_copy(
            src_ref=acc.at[step], dst_ref=part.at[me],
            send_sem=red_out.at[step], recv_sem=red_in.at[me],
            device_id={"tm": lax.rem(me + step, n)}, device_id_type=MESH,
        )

    def lag_parts(near, act):
        for step in range(n - 1, 0, -1):
            @pl.when((me + step < n) & (straight(step // 2, chip) == near))
            def _(step=step):
                act(lag_part(step))

    lag_parts(True, start)

    far_forwards(0, start, True)
    for c in range(chunks):
        if c + 1 < chunks:
            far_forwards(c + 1, start, True)
        take(c, 1)

        def far_images(step, c=c):
            r = lax.rem(row + 1 + lax.div(step, max(1, cols - 1)), rows)
            q = lax.rem(col + 1 + lax.rem(step, max(1, cols - 1)), cols)
            source = r * cols + q

            @pl.when(need(2 * source, chip))
            def _():
                image = image_of(far[c, pl.ds(2 * source, 2)], c)
                if c == 0:
                    acc[pl.ds(2 * source, 2)] = image
                else:
                    acc[pl.ds(2 * source, 2)] += image

        each(0, (rows - 1) * (cols - 1), far_images)

    lag_parts(False, start)

    for c in range(chunks):
        sends(c, wait_send)
        relays(c, wait_send, False)
        forwards(c, wait_send, False)
        far_forwards(c, wait_send, False)

    def add_lag(lag, value):
        pltpu.make_async_remote_copy(
            src_ref=acc.at[0], dst_ref=part.at[lag],
            send_sem=red_out.at[0], recv_sem=red_in.at[lag],
            device_id={"tm": pair}, device_id_type=MESH,
        ).wait_recv()
        return value + part[lag]

    value = lax.fori_loop(0, me, add_lag, acc[0])
    for j in range(m):
        total[j] = value[:, j * share_size:(j + 1) * share_size]

    def to_floor(step):
        other = lax.rem(floor + step, m)
        return pltpu.make_async_remote_copy(
            src_ref=total.at[other], dst_ref=share.at[floor],
            send_sem=floor_out.at[step], recv_sem=floor_in.at[floor],
            device_id={"floor": other}, device_id_type=MESH,
        )

    for step in range(m - 1, 0, -1):
        to_floor(step).start()
    result = total[floor]
    for step in range(1, m):
        source = lax.rem(floor + step, m)
        pltpu.make_async_remote_copy(
            src_ref=total.at[source], dst_ref=share.at[source],
            send_sem=floor_out.at[step], recv_sem=floor_in.at[source],
            device_id={"floor": source}, device_id_type=MESH,
        ).wait_recv()
        result = result + share[source]
    out_ref[0] = result.astype(out_ref.dtype)

    lag_parts(True, wait_send)
    lag_parts(False, wait_send)
    for step in range(1, m):
        to_floor(step).wait_send()


def square(
    m, widths, split, x_hbm, op_hbm, out_ref, x, mine, op, acc, sums, part, total, share,
    load_sem, swap_in, pair_in, in_sem, sent, red_in, floor_in, hello,
):
    n = part.shape[0]
    chips = n // 2
    me, floor = lax.axis_index("tm"), lax.axis_index("floor")
    chip, core = lax.div(me, 2), lax.rem(me, 2)
    row, col = lax.div(chip, 2), lax.rem(chip, 2)
    sources = [chip, 2 * row + 1 - col, 2 * (1 - row) + col, 2 * (1 - row) + 1 - col]
    other = 1 - core
    pair = 2 * chip + other
    chunks, starts = len(widths), [sum(widths[:j]) for j in range(len(widths))]
    k, depth = x.shape[1], x.shape[2]
    sensors = op.shape[1]
    share_size = sensors // m
    inner = (chip == 1) | (chip == 2)

    def columns(half, j):
        begin, size = (starts[j], widths[j]) if isinstance(j, int) else (j * widths[0], widths[0])
        return pl.ds(pl.multiple_of(half * depth + begin, 128), size)

    def at(j):
        if isinstance(j, int):
            return slice(starts[j], starts[j] + widths[j])
        return pl.ds(pl.multiple_of(j * widths[0], 128), widths[0])

    own = pltpu.make_async_copy(x_hbm.at[0, :, pl.ds(pl.multiple_of(core * depth, 128), depth)], x.at[core], load_sem.at[0])
    staged = pltpu.make_async_copy(x_hbm.at[0], mine, load_sem.at[1])
    weights = pltpu.make_async_copy(
        op_hbm.at[0, :, pl.ds(pl.multiple_of(core * depth, 128), depth)], op.at[core], load_sem.at[2]
    )
    staged.start()
    own.start()

    neighbours = (2 * sources[1], 2 * sources[1] + 1, 2 * sources[2], 2 * sources[2] + 1)

    def greet(sem, all_round):
        pl.semaphore_signal(sem, inc=1, device_id={"tm": pair}, device_id_type=MESH)

        @pl.when(all_round)
        def _():
            for target in neighbours:
                pl.semaphore_signal(sem, inc=1, device_id={"tm": target}, device_id_type=MESH)

        @pl.when(floor > 0)
        def _():
            pl.semaphore_signal(sem, inc=1, device_id={"floor": floor - 1}, device_id_type=MESH)

        @pl.when(floor < m - 1)
        def _():
            pl.semaphore_signal(sem, inc=1, device_id={"floor": floor + 1}, device_id_type=MESH)

    beside = jnp.where(floor > 0, 1, 0) + jnp.where(floor < m - 1, 1, 0)
    greeted = 5 + beside
    barrier = pltpu.get_barrier_semaphore()
    greet(barrier, chip < chips - 1)
    pl.semaphore_wait(barrier, jnp.where(inner, 3, 5) + beside)

    @pl.when(chip == chips - 1)
    def _():
        for target in neighbours:
            pl.semaphore_signal(hello.at[2], inc=1, device_id={"tm": target}, device_id_type=MESH)

    def need(source, at):
        return source + at < chips

    needs = [need(source, chip) for source in sources]

    def by_x(source, parity, j):
        outer = (source == 0) | (source == chips - 1)
        through_first = jnp.where(source == 1, j < split, j >= split)
        return (outer & (parity == j % 2)) | (jnp.logical_not(outer) & through_first)

    def remote(src, dst, out, into, target):
        return pltpu.make_async_remote_copy(
            src_ref=src, dst_ref=dst, send_sem=out, recv_sem=into, device_id={"tm": target}, device_id_type=MESH
        )

    def start(copy):
        copy.start()

    def wait_send(copy):
        copy.wait_send()

    def send_x(j, act):
        @pl.when(needs_at_x | by_x(chip, core, j))
        def _():
            for half in (0, 1):
                act(remote(mine.at[:, columns(half, j)], x.at[2 + core, :, at(j)], sent.at[0], in_sem.at[1, j], 2 * sources[1] + half))

    def send_y(j, act):
        @pl.when(needs_at_y | jnp.logical_not(by_x(chip, core, j)))
        def _():
            for half in (0, 1):
                act(remote(mine.at[:, columns(half, j)], x.at[4 + core, :, at(j)], sent.at[0], in_sem.at[2, j], 2 * sources[2] + half))

    needs_at_x, needs_at_y = need(chip, sources[1]), need(chip, sources[2])

    def send_pair(act):
        there = pl.ds(pl.multiple_of(other * depth, 128), depth)
        act(remote(mine.at[:, there], x.at[core], sent.at[0], pair_in.at[0], pair))

    parts = (slice(0, starts[2]), slice(starts[2], depth))

    def swap(p, act):
        begin, size = parts[p].start, parts[p].stop - parts[p].start
        there = pl.ds(pl.multiple_of(other * depth + begin, 128), size)
        act(remote(op_hbm.at[0, :, there], op.at[core, :, parts[p]], sent.at[0], swap_in.at[p], pair))

    def swapped(p):
        remote(op.at[core, :, parts[p]], op.at[other, :, parts[p]], sent.at[0], swap_in.at[p], pair).wait_recv()

    def taken(source, j, blocks):
        here = x.at[2 * source:2 * source + blocks, :, at(j)]
        remote(here, here, sent.at[0], in_sem.at[source, j], pair).wait_recv()

    def pass_x(j, parity, act):
        act(remote(x.at[2 + parity, :, at(j)], x.at[6 + parity, :, at(j)], sent.at[0], in_sem.at[3, j], 2 * sources[2] + core))

    def pass_y(j, parity, act):
        act(remote(x.at[4 + parity, :, at(j)], x.at[6 + parity, :, at(j)], sent.at[0], in_sem.at[3, j], 2 * sources[1] + core))

    def come(source, j, both, onward):
        count = onward[0].astype(jnp.int32) + onward[1].astype(jnp.int32)
        for blocks in (1, 2):
            @pl.when(jnp.where(both, 2, count) == blocks)
            def _(blocks=blocks):
                taken(source, j, blocks)

    def from_x(j, here, wait, act):
        onward = [by_x(sources[1], parity, j) for parity in (0, 1)]

        @pl.when(here)
        def _():
            if wait:
                come(1, j, needs[1], onward)
            for parity in (0, 1):
                @pl.when(onward[parity])
                def _(parity=parity):
                    pass_x(j, parity, act)

    def from_y(j, here, wait, act):
        onward = [jnp.logical_not(by_x(sources[2], parity, j)) for parity in (0, 1)]

        @pl.when(here)
        def _():
            if wait:
                come(2, j, needs[2], onward)
            for parity in (0, 1):
                @pl.when(onward[parity])
                def _(parity=parity):
                    pass_y(j, parity, act)

    lead = chunks // 2
    staged.wait()
    for j in range(lead):
        @pl.when(needs_at_x)
        def _(j=j):
            send_x(j, start)

        @pl.when(needs_at_y)
        def _(j=j):
            send_y(j, start)

    def send_only_across():
        for j in range(chunks):
            @pl.when(jnp.logical_not(needs_at_x))
            def _(j=j):
                send_x(j, start)

            @pl.when(jnp.logical_not(needs_at_y))
            def _(j=j):
                send_y(j, start)

    @pl.when(chip == chips - 1)
    def _():
        send_only_across()

    weights.start()
    send_pair(start)
    for p in (0, 1):
        swap(p, start)

    @pl.when(inner)
    def _():
        pl.semaphore_wait(hello.at[2], 2)
        send_only_across()

    greet(hello.at[0], True)

    def send_late(j):
        @pl.when(needs_at_x)
        def _():
            send_x(j, start)

        @pl.when(needs_at_y)
        def _():
            send_y(j, start)

    for j in range(chunks):
        from_x(j, jnp.logical_not(needs[1]), True, start)
        from_y(j, jnp.logical_not(needs[2]), True, start)
        for late in range(lead, chunks):
            if j == min(2 * (late - lead) + 1, chunks - 1):
                @pl.when(inner)
                def _(late=late):
                    send_late(late)

    pl.semaphore_wait(hello.at[0], greeted)
    greet(hello.at[1], True)

    def arrive(j):
        from_x(j, needs[1], True, start)
        from_y(j, needs[2], True, start)
        if j == split - 1:
            @pl.when(jnp.logical_not(inner))
            def _():
                for late in range(lead, chunks):
                    send_late(late)

    first = chip == 0

    def ready(j, step):
        if step == 0:
            own.wait()
            weights.wait()
            remote(x.at[other], x.at[other], sent.at[0], pair_in.at[0], pair).wait_recv()
            swapped(0)
        if step == 2:
            swapped(1)
        taken(3, j, 2)

    def multiply(j, pieces):
        rows = jnp.concatenate([x[p, :, at(j)] for p in pieces], axis=0)
        depth_here = rows.shape[-1]
        return lax.dot_general(
            rows.reshape(-1, depth_here), op[:, :, at(j)].reshape(-1, depth_here), (((1,), (1,)), ((), ())),
            preferred_element_type=jnp.float32,
        ).reshape(-1, k, 2 * sensors)

    def compute(j, begin=False):
        image = multiply(j, [slice(None)])
        if begin:
            acc[...] = image
        else:
            acc[...] += image

    def compute_far(j):
        image = multiply(j, [slice(0, 2), slice(6, 8)])
        acc[0:2] += image[0:2]
        acc[6:8] += image[2:4]

    def compute_near(j):
        acc[2:6] += multiply(j, [slice(2, 6)])

    def slot_of(block):
        source = block // 2
        across = jnp.where(col == source % 2, 0, 2) + jnp.where(row == source // 2, 0, 4)
        return across + block % 2

    def place(i):
        return jnp.where(2 * floor >= m, i, m - 1 - i)

    def record(u, j, act):
        act(pltpu.make_async_remote_copy(
            src_ref=sums.at[u, j], dst_ref=part.at[me, j], send_sem=sent.at[1], recv_sem=red_in.at[j],
            device_id={"tm": jnp.minimum(2 * chip + u, n - 1)}, device_id_type=MESH,
        ))

    def records(places, act, add):
        def one(i, _):
            j = place(i)
            here = pl.ds(pl.multiple_of(j * share_size, share_size), share_size)
            there = pl.ds(pl.multiple_of(sensors + j * share_size, share_size), share_size)
            for u in places:
                @pl.when(2 * chip + u < n)
                def _(u=u):
                    if add:
                        value = acc[slot_of(u), :, here]
                        if u > 0:
                            value = value + acc[slot_of(u - 1), :, there]
                        sums[u, j] = value
                    if u > 1:
                        record(u, j, act)
                    else:
                        @pl.when(core != u)
                        def _():
                            record(u, j, act)

            return 0

        lax.fori_loop(0, m, one, 0)

    arrive(0)
    arrive(1)
    swapped_order = jnp.where(inner, 1, 0)
    for step in range(chunks - 1):
        if step > 0:
            @pl.when(jnp.logical_not(first))
            def _(step=step):
                arrive(step + 1)

            if step > 1:
                @pl.when(first)
                def _(step=step):
                    arrive(step)

        j = (swapped_order, 1 - swapped_order)[step] if step < 2 else step
        ready(j, step)
        compute(j, step == 0)

    ready(chunks - 1, chunks - 1)
    pl.semaphore_wait(hello.at[1], greeted)

    @pl.when(first)
    def _():
        compute_far(chunks - 1)
        records((7, 1, 0), start, True)
        arrive(chunks - 1)
        compute_near(chunks - 1)
        records((6, 5, 3, 4, 2), start, True)

    @pl.when(jnp.logical_not(first))
    def _():
        compute(chunks - 1)
        records(range(n - 1, -1, -1), start, True)


    for j in range(chunks):
        send_x(j, wait_send)
        send_y(j, wait_send)
        from_x(j, True, False, wait_send)
        from_y(j, True, False, wait_send)
    send_pair(wait_send)
    for p in (0, 1):
        swap(p, wait_send)

    def to_floor(other, act):
        act(pltpu.make_async_remote_copy(
            src_ref=total.at[other], dst_ref=share.at[floor],
            send_sem=sent.at[2], recv_sem=floor_in.at[0],
            device_id={"floor": other}, device_id_type=MESH,
        ))

    def gather_share(i, _):
        j = place(i)

        for c in range(chips):
            @pl.when(chip == c)
            def _(c=c):
                pltpu.make_async_remote_copy(
                    src_ref=sums.at[0:2 * c + 1, j], dst_ref=part.at[0:2 * c + 1, j], send_sem=sent.at[1],
                    recv_sem=red_in.at[j], device_id={"tm": pair}, device_id_type=MESH,
                ).wait_recv()

        def add_part(p, value):
            return value + part[jnp.where(p == 0, pair, 2 * chip - p), j]

        total[j] = lax.fori_loop(0, 2 * chip + 1, add_part, sums[core, j])

        @pl.when(j != floor)
        def _():
            to_floor(j, start)

        return 0

    lax.fori_loop(0, m, gather_share, 0)
    records(range(n - 1, -1, -1), wait_send, False)
    for step in range(1, m):
        to_floor(lax.rem(floor + step, m), wait_send)
    everyone = pl.ds(0, m - 1)
    pltpu.make_async_remote_copy(
        src_ref=total.at[everyone], dst_ref=share.at[everyone], send_sem=sent.at[2], recv_sem=floor_in.at[0],
        device_id={"floor": lax.rem(floor + 1, m)}, device_id_type=MESH,
    ).wait_recv()
    result = total[floor]
    for step in range(1, m):
        result = result + share[lax.rem(floor + step, m)]
    out_ref[0] = result.astype(out_ref.dtype)


def square_call(n, m, samples, operator):
    _, k, depth = samples.shape
    sensors = operator.shape[1]
    half = depth // 2
    widths = [part * half // 16 for part in (5, 5, 4, 2)]
    chunks = len(widths)
    dma = pltpu.SemaphoreType.DMA
    return pl.pallas_call(
        functools.partial(square, m, widths, 1),
        out_shape=pltpu.VMEM((1, k, sensors // m), jnp.bfloat16),
        in_specs=[pl.BlockSpec(memory_space=pl.ANY)] * 2,
        out_specs=pl.BlockSpec(memory_space=pltpu.VMEM),
        scratch_shapes=[
            pltpu.VMEM((n, k, half), jnp.bfloat16),
            pltpu.VMEM((k, depth), jnp.bfloat16),
            pltpu.VMEM((2, sensors, half), jnp.bfloat16),
            pltpu.VMEM((n, k, 2 * sensors), jnp.float32),
            pltpu.VMEM((n, m, k, sensors // m), jnp.float32),
            pltpu.VMEM((n, m, k, sensors // m), jnp.float32),
            pltpu.VMEM((m, k, sensors // m), jnp.float32),
            pltpu.VMEM((m, k, sensors // m), jnp.float32),
            dma((3,)), dma((2,)), dma((1,)), dma((4, chunks)), dma((3,)), dma((m,)), dma((1,)),
            pltpu.SemaphoreType.REGULAR((3,)),
        ],
        compiler_params=pltpu.CompilerParams(collective_id=0, has_side_effects=True),
    )(samples, operator)


def solution(mesh):
    n, m = mesh.shape["tm"], mesh.shape["floor"]

    def local(samples, operator):
        if grid_of(n // 2) == (2, 2):
            return square_call(n, m, samples, operator)
        _, k, depth = samples.shape
        sensors = operator.shape[1]
        chunks = 4
        width = depth // chunks
        return pl.pallas_call(
            functools.partial(kernel, n, m, chunks),
            out_shape=pltpu.VMEM((1, k, sensors // m), jnp.bfloat16),
            in_specs=[pl.BlockSpec(memory_space=pl.ANY)] * 2,
            out_specs=pl.BlockSpec(memory_space=pltpu.VMEM),
            scratch_shapes=[
                pltpu.VMEM((chunks, n, k, width), jnp.bfloat16),
                pltpu.VMEM((chunks, n, k, width), jnp.bfloat16),
                pltpu.VMEM((chunks, sensors, width), jnp.bfloat16),
                pltpu.VMEM((n, k, sensors), jnp.float32),
                pltpu.VMEM((n, k, sensors), jnp.float32),
                pltpu.VMEM((m, k, sensors // m), jnp.float32),
                pltpu.VMEM((m, k, sensors // m), jnp.float32),
                pltpu.SemaphoreType.DMA((chunks,)),
                pltpu.SemaphoreType.DMA((chunks,)),
                pltpu.SemaphoreType.DMA((chunks, n // 2)),
                pltpu.SemaphoreType.DMA((chunks,)),
                pltpu.SemaphoreType.DMA((chunks, n // 2)),
                pltpu.SemaphoreType.DMA((chunks, n // 2, max(1, max(grid_of(n // 2)) - 1))),
                pltpu.SemaphoreType.DMA((chunks, n)),
                pltpu.SemaphoreType.DMA((n,)),
                pltpu.SemaphoreType.DMA((n,)),
                pltpu.SemaphoreType.DMA((m,)),
                pltpu.SemaphoreType.DMA((m,)),
            ],
            compiler_params=pltpu.CompilerParams(collective_id=0, has_side_effects=True),
        )(samples, operator)

    placed = (P("tm", None, "floor"), P("tm", None, "floor"))
    return jax.shard_map(
        local, mesh=mesh, in_specs=placed, out_specs=P("tm", None, "floor"), check_vma=False
    )
```

```python
import functools

import jax
import jax.numpy as jnp
from jax import lax
from jax.experimental import pallas as pl
from jax.experimental.pallas import tpu as pltpu
from jax.sharding import PartitionSpec as P

MESH = pl.DeviceIdType.MESH
LOOK = 1


def each(low, high, body):
    if high - low <= 4:
        for i in range(low, high):
            body(i)
    else:
        def step(i, carry):
            body(i)
            return carry

        lax.fori_loop(low, high, step, 0)


def grid_of(chips):
    rows = 1
    while rows * rows * 4 <= chips and chips % (rows * 2) == 0:
        rows *= 2
    return rows, chips // rows


def kernel(
    n, m, chunks, x_hbm, op_hbm, out_ref, x, far, op, acc, part, total, share,
    own_sem, op_sem, out_sem, pair_sem, fwd_sem, relay_sem, in_sem,
    red_out, red_in, floor_out, floor_in,
):
    me, floor = lax.axis_index("tm"), lax.axis_index("floor")
    chips = n // 2
    rows, cols = grid_of(chips)
    chip, core = lax.div(me, 2), lax.rem(me, 2)
    row, col = lax.div(chip, cols), lax.rem(chip, cols)
    pair = 2 * chip + 1 - core
    k, width = x.shape[2], x.shape[3]
    sensors = op.shape[1]
    share_size = sensors // m

    def columns(c):
        return pl.ds(c * width, width)

    own = [pltpu.make_async_copy(x_hbm.at[0, :, columns(c)], x.at[c, me], own_sem.at[c]) for c in range(chunks)]
    weights = [pltpu.make_async_copy(op_hbm.at[0, :, columns(c)], op.at[c], op_sem.at[c]) for c in range(chunks)]
    for c in range(chunks):
        own[c].start()
        weights[c].start()

    barrier = pltpu.get_barrier_semaphore()
    for step in range(1, n):
        pl.semaphore_signal(barrier, inc=1, device_id={"tm": lax.rem(me + step, n)}, device_id_type=MESH)
    for step in range(1, m):
        pl.semaphore_signal(barrier, inc=1, device_id={"floor": lax.rem(floor + step, m)}, device_id_type=MESH)
    pl.semaphore_wait(barrier, n + m - 2)

    def need(block, at_chip):
        return 2 * at_chip + block < n

    many = max(rows, cols)

    def straight(source, at):
        return (lax.div(source, cols) == lax.div(at, cols)) | (lax.rem(source, cols) == lax.rem(at, cols))

    def relayed(odd, source, block, at, step):
        turn = lax.rem(core + odd, 2) == 0
        r, q = lax.div(source, cols), lax.rem(source, cols)
        r_at, q_at = lax.div(at, cols), lax.rem(at, cols)
        r_to, q_to = lax.rem(r + step, rows), lax.rem(q + step, cols)
        down = (r_at == r) & (step < rows) & (turn | ((r_to == 0) & (q == 0)))
        along = (q_at == q) & (step < cols) & (jnp.logical_not(turn) | ((q_to == 0) & (r == 0)))
        target = jnp.where(r_at == r, r_to * cols + q_at, r_at * cols + q_to)
        return (at != 0) & (down | along) & need(block, target), 2 * target + core

    def route(odd, source, block, at):
        passes = at < 0
        for step in range(1, many):
            passes = passes | relayed(odd, source, block, at, step)[0]
        return straight(source, at) & (need(block, at) | passes), passes

    def make_plan(step, odd):
        other = lax.rem(chip + step, chips)
        block = 2 * other + core
        wanted, _ = route(odd, chip, me, other)
        _, passes = route(odd, other, block, chip)
        near = straight(other, chip)
        here = need(block, chip) & near, need(block, chip) & jnp.logical_not(near)
        alone = here[0] & jnp.logical_not(passes)
        onward = [relayed(odd, other, block, chip, s) for s in range(1, many)]
        return other, block, wanted, passes, here, alone, onward

    plans = {}
    if chips <= 5:
        plans = {(step, odd): make_plan(step, odd) for step in range(1, chips) for odd in (0, 1)}

    def plan(step, c):
        return plans[step, c % 2] if plans else make_plan(step, c % 2)

    others = [2 * lax.rem(chip + step, chips) + 1 - core for step in range(chips)] if plans else None
    def other_here(block):
        near = straight(lax.div(block, 2), chip)
        return need(block, chip) & near, need(block, chip) & jnp.logical_not(near)

    others_here = [other_here(block) for block in others] if plans else None
    self_here = need(me, chip)

    busy = need(2 * row * cols, chip) | need(2 * col, chip)

    def send(c, block, target, sem, source=None, into=None):
        return pltpu.make_async_remote_copy(
            src_ref=x.at[c, block] if source is None else source,
            dst_ref=(x if into is None else into).at[c, block],
            send_sem=sem, recv_sem=in_sem.at[c, block], device_id={"tm": target}, device_id_type=MESH,
        )

    def mine(c):
        return x_hbm.at[0, :, columns(c)]

    def sends(c, act):
        def one(step):
            _, block, wanted, *_ = plan(step, c)

            @pl.when(wanted)
            def _():
                act(send(c, me, block, out_sem.at[c, step], mine(c)))

        each(1, chips, one)

        @pl.when(self_here)
        def _():
            act(send(c, me, pair, pair_sem.at[c], mine(c)))

    def relays(c, act, wait):
        def one(step):
            source, block, _, passes, _, _, onward = plan(step, c)

            @pl.when(passes)
            def _():
                if wait:
                    send(c, block, pair, fwd_sem.at[c, source]).wait_recv()
                for s, (wanted, target) in enumerate(onward):
                    @pl.when(wanted)
                    def _(s=s, target=target):
                        act(send(c, block, target, relay_sem.at[c, source, s], None, far))

        each(1, chips, one)

    def forwards(c, act, wait):
        def one(step):
            source, block, _, _, here, alone, _ = plan(step, c)
            if wait:
                @pl.when(alone)
                def _():
                    send(c, block, pair, fwd_sem.at[c, source]).wait_recv()

            @pl.when(here[0])
            def _():
                act(send(c, block, pair, fwd_sem.at[c, source]))

        each(1, chips, one)

    def far_forwards(c, act, wait):
        def one(step):
            source, block, _, _, here, _, _ = plan(step, c)

            @pl.when(here[1])
            def _():
                copy = send(c, block, pair, fwd_sem.at[c, source], far.at[c, block], far)
                if wait:
                    copy.wait_recv()
                act(copy)

        each(1, chips, one)

    def take(c, part_of):
        def one(step):
            block = others[step] if plans else 2 * lax.rem(chip + step, chips) + 1 - core
            here = (others_here[step] if plans else other_here(block))[part_of]

            @pl.when(here)
            def _():
                send(c, block, pair, pair_sem.at[c], None, far if part_of else None).wait_recv()

        each(0, chips, one)

    def start(copy):
        copy.start()

    def wait_send(copy):
        copy.wait_send()


    tile = min(n, max(1, 128 // k))

    def image_of(block_rows, c):
        return lax.dot_general(
            block_rows.reshape(-1, width), op[c], (((1,), (1,)), ((), ())), preferred_element_type=jnp.float32
        ).reshape(-1, k, sensors)

    for c in range(chunks):
        sends(c, start)
    for c in range(min(LOOK, chunks)):
        relays(c, start, True)
    forwards(0, start, True)
    for c in range(chunks):
        if c + LOOK < chunks:
            relays(c + LOOK, start, True)
        if c + 1 < chunks:
            forwards(c + 1, start, True)
        take(c, 0)
        own[c].wait()
        weights[c].wait()

        @pl.when(busy)
        def _(c=c):
            for r in range(n // tile):
                image = image_of(x[c, r * tile:(r + 1) * tile], c)
                if c == 0:
                    acc[r * tile:(r + 1) * tile] = image
                else:
                    acc[r * tile:(r + 1) * tile] += image

    def lag_part(step):
        return pltpu.make_async_remote_copy(
            src_ref=acc.at[step], dst_ref=part.at[me],
            send_sem=red_out.at[step], recv_sem=red_in.at[me],
            device_id={"tm": lax.rem(me + step, n)}, device_id_type=MESH,
        )

    def lag_parts(near, act):
        for step in range(n - 1, 0, -1):
            @pl.when((me + step < n) & (straight(step // 2, chip) == near))
            def _(step=step):
                act(lag_part(step))

    lag_parts(True, start)

    far_forwards(0, start, True)
    for c in range(chunks):
        if c + 1 < chunks:
            far_forwards(c + 1, start, True)
        take(c, 1)

        def far_images(step, c=c):
            r = lax.rem(row + 1 + lax.div(step, max(1, cols - 1)), rows)
            q = lax.rem(col + 1 + lax.rem(step, max(1, cols - 1)), cols)
            source = r * cols + q

            @pl.when(need(2 * source, chip))
            def _():
                image = image_of(far[c, pl.ds(2 * source, 2)], c)
                if c == 0:
                    acc[pl.ds(2 * source, 2)] = image
                else:
                    acc[pl.ds(2 * source, 2)] += image

        each(0, (rows - 1) * (cols - 1), far_images)

    lag_parts(False, start)

    for c in range(chunks):
        sends(c, wait_send)
        relays(c, wait_send, False)
        forwards(c, wait_send, False)
        far_forwards(c, wait_send, False)

    def add_lag(lag, value):
        pltpu.make_async_remote_copy(
            src_ref=acc.at[0], dst_ref=part.at[lag],
            send_sem=red_out.at[0], recv_sem=red_in.at[lag],
            device_id={"tm": pair}, device_id_type=MESH,
        ).wait_recv()
        return value + part[lag]

    value = lax.fori_loop(0, me, add_lag, acc[0])
    for j in range(m):
        total[j] = value[:, j * share_size:(j + 1) * share_size]

    def to_floor(step):
        other = lax.rem(floor + step, m)
        return pltpu.make_async_remote_copy(
            src_ref=total.at[other], dst_ref=share.at[floor],
            send_sem=floor_out.at[step], recv_sem=floor_in.at[floor],
            device_id={"floor": other}, device_id_type=MESH,
        )

    for step in range(m - 1, 0, -1):
        to_floor(step).start()
    result = total[floor]
    for step in range(1, m):
        source = lax.rem(floor + step, m)
        pltpu.make_async_remote_copy(
            src_ref=total.at[source], dst_ref=share.at[source],
            send_sem=floor_out.at[step], recv_sem=floor_in.at[source],
            device_id={"floor": source}, device_id_type=MESH,
        ).wait_recv()
        result = result + share[source]
    out_ref[0] = result.astype(out_ref.dtype)

    lag_parts(True, wait_send)
    lag_parts(False, wait_send)
    for step in range(1, m):
        to_floor(step).wait_send()


def square(
    m, widths, split, x_hbm, op_hbm, out_ref, x, mine, op, acc, sums, part, total, share,
    load_sem, swap_in, pair_in, in_sem, sent, red_in, floor_in, hello,
):
    n = part.shape[0]
    chips = n // 2
    me, floor = lax.axis_index("tm"), lax.axis_index("floor")
    chip, core = lax.div(me, 2), lax.rem(me, 2)
    row, col = lax.div(chip, 2), lax.rem(chip, 2)
    sources = [chip, 2 * row + 1 - col, 2 * (1 - row) + col, 2 * (1 - row) + 1 - col]
    other = 1 - core
    pair = 2 * chip + other
    chunks, starts = len(widths), [sum(widths[:j]) for j in range(len(widths))]
    k, depth = x.shape[1], x.shape[2]
    sensors = op.shape[1]
    share_size = sensors // m
    inner = (chip == 1) | (chip == 2)

    def columns(half, j):
        begin, size = (starts[j], widths[j]) if isinstance(j, int) else (j * widths[0], widths[0])
        return pl.ds(pl.multiple_of(half * depth + begin, 128), size)

    def at(j):
        if isinstance(j, int):
            return slice(starts[j], starts[j] + widths[j])
        return pl.ds(pl.multiple_of(j * widths[0], 128), widths[0])

    own = pltpu.make_async_copy(x_hbm.at[0, :, pl.ds(pl.multiple_of(core * depth, 128), depth)], x.at[core], load_sem.at[0])
    staged = pltpu.make_async_copy(x_hbm.at[0], mine, load_sem.at[1])
    weights = pltpu.make_async_copy(
        op_hbm.at[0, :, pl.ds(pl.multiple_of(core * depth, 128), depth)], op.at[core], load_sem.at[2]
    )
    staged.start()
    own.start()

    neighbours = (2 * sources[1], 2 * sources[1] + 1, 2 * sources[2], 2 * sources[2] + 1)

    def greet(sem, all_round):
        pl.semaphore_signal(sem, inc=1, device_id={"tm": pair}, device_id_type=MESH)

        @pl.when(all_round)
        def _():
            for target in neighbours:
                pl.semaphore_signal(sem, inc=1, device_id={"tm": target}, device_id_type=MESH)

        @pl.when(floor > 0)
        def _():
            pl.semaphore_signal(sem, inc=1, device_id={"floor": floor - 1}, device_id_type=MESH)

        @pl.when(floor < m - 1)
        def _():
            pl.semaphore_signal(sem, inc=1, device_id={"floor": floor + 1}, device_id_type=MESH)

    beside = jnp.where(floor > 0, 1, 0) + jnp.where(floor < m - 1, 1, 0)
    greeted = 5 + beside
    barrier = pltpu.get_barrier_semaphore()
    greet(barrier, chip < chips - 1)
    pl.semaphore_wait(barrier, jnp.where(inner, 3, 5) + beside)

    @pl.when(chip == chips - 1)
    def _():
        for target in neighbours:
            pl.semaphore_signal(hello.at[2], inc=1, device_id={"tm": target}, device_id_type=MESH)

    def need(source, at):
        return source + at < chips

    needs = [need(source, chip) for source in sources]

    def by_x(source, parity, j):
        outer = (source == 0) | (source == chips - 1)
        through_first = jnp.where(source == 1, j < split, j >= split)
        return (outer & (parity == j % 2)) | (jnp.logical_not(outer) & through_first)

    def remote(src, dst, out, into, target):
        return pltpu.make_async_remote_copy(
            src_ref=src, dst_ref=dst, send_sem=out, recv_sem=into, device_id={"tm": target}, device_id_type=MESH
        )

    def start(copy):
        copy.start()

    def wait_send(copy):
        copy.wait_send()

    def send_x(j, act):
        @pl.when(needs_at_x | by_x(chip, core, j))
        def _():
            for half in (0, 1):
                act(remote(mine.at[:, columns(half, j)], x.at[2 + core, :, at(j)], sent.at[0], in_sem.at[1, j], 2 * sources[1] + half))

    def send_y(j, act):
        @pl.when(needs_at_y | jnp.logical_not(by_x(chip, core, j)))
        def _():
            for half in (0, 1):
                act(remote(mine.at[:, columns(half, j)], x.at[4 + core, :, at(j)], sent.at[0], in_sem.at[2, j], 2 * sources[2] + half))

    needs_at_x, needs_at_y = need(chip, sources[1]), need(chip, sources[2])

    def send_pair(act):
        there = pl.ds(pl.multiple_of(other * depth, 128), depth)
        act(remote(mine.at[:, there], x.at[core], sent.at[0], pair_in.at[0], pair))

    parts = (slice(0, starts[2]), slice(starts[2], depth))

    def swap(p, act):
        begin, size = parts[p].start, parts[p].stop - parts[p].start
        there = pl.ds(pl.multiple_of(other * depth + begin, 128), size)
        act(remote(op_hbm.at[0, :, there], op.at[core, :, parts[p]], sent.at[0], swap_in.at[p], pair))

    def swapped(p):
        remote(op.at[core, :, parts[p]], op.at[other, :, parts[p]], sent.at[0], swap_in.at[p], pair).wait_recv()

    def taken(source, j, blocks):
        here = x.at[2 * source:2 * source + blocks, :, at(j)]
        remote(here, here, sent.at[0], in_sem.at[source, j], pair).wait_recv()

    def pass_x(j, parity, act):
        act(remote(x.at[2 + parity, :, at(j)], x.at[6 + parity, :, at(j)], sent.at[0], in_sem.at[3, j], 2 * sources[2] + core))

    def pass_y(j, parity, act):
        act(remote(x.at[4 + parity, :, at(j)], x.at[6 + parity, :, at(j)], sent.at[0], in_sem.at[3, j], 2 * sources[1] + core))

    def come(source, j, both, onward):
        count = onward[0].astype(jnp.int32) + onward[1].astype(jnp.int32)
        for blocks in (1, 2):
            @pl.when(jnp.where(both, 2, count) == blocks)
            def _(blocks=blocks):
                taken(source, j, blocks)

    def from_x(j, here, wait, act):
        onward = [by_x(sources[1], parity, j) for parity in (0, 1)]

        @pl.when(here)
        def _():
            if wait:
                come(1, j, needs[1], onward)
            for parity in (0, 1):
                @pl.when(onward[parity])
                def _(parity=parity):
                    pass_x(j, parity, act)

    def from_y(j, here, wait, act):
        onward = [jnp.logical_not(by_x(sources[2], parity, j)) for parity in (0, 1)]

        @pl.when(here)
        def _():
            if wait:
                come(2, j, needs[2], onward)
            for parity in (0, 1):
                @pl.when(onward[parity])
                def _(parity=parity):
                    pass_y(j, parity, act)

    lead = chunks // 2
    staged.wait()
    for j in range(chunks):
        at_once = jnp.logical_not(inner) | (j < lead)

        @pl.when(at_once & needs_at_x)
        def _(j=j):
            send_x(j, start)

        @pl.when(at_once & needs_at_y)
        def _(j=j):
            send_y(j, start)

    def send_only_across():
        for j in range(chunks):
            @pl.when(jnp.logical_not(needs_at_x))
            def _(j=j):
                send_x(j, start)

            @pl.when(jnp.logical_not(needs_at_y))
            def _(j=j):
                send_y(j, start)

    @pl.when(chip == chips - 1)
    def _():
        send_only_across()

    weights.start()
    send_pair(start)
    for p in (0, 1):
        swap(p, start)

    @pl.when(inner)
    def _():
        pl.semaphore_wait(hello.at[2], 2)
        send_only_across()

    greet(hello.at[0], True)

    def send_late(j):
        @pl.when(needs_at_x)
        def _():
            send_x(j, start)

        @pl.when(needs_at_y)
        def _():
            send_y(j, start)

    for j in range(chunks):
        from_x(j, jnp.logical_not(needs[1]), True, start)
        from_y(j, jnp.logical_not(needs[2]), True, start)
        for late in range(lead, chunks):
            if j == min(2 * (late - lead) + 1, chunks - 1):
                @pl.when(inner)
                def _(late=late):
                    send_late(late)

    pl.semaphore_wait(hello.at[0], greeted)
    greet(hello.at[1], True)

    def arrive(j):
        from_x(j, needs[1], True, start)
        from_y(j, needs[2], True, start)
    first = chip == 0

    def ready(j):
        if j == 0:
            own.wait()
            weights.wait()
            remote(x.at[other], x.at[other], sent.at[0], pair_in.at[0], pair).wait_recv()
            swapped(0)
        if j == 2:
            swapped(1)

    def multiply(j, pieces):
        rows = jnp.concatenate([x[p, :, at(j)] for p in pieces], axis=0)
        depth_here = rows.shape[-1]
        return lax.dot_general(
            rows.reshape(-1, depth_here), op[:, :, at(j)].reshape(-1, depth_here), (((1,), (1,)), ((), ())),
            preferred_element_type=jnp.float32,
        ).reshape(-1, k, 2 * sensors)

    def compute(j, low, high, begin):
        image = multiply(j, [slice(low, high)])
        if begin:
            acc[low:high] = image
        else:
            acc[low:high] += image

    def compute_ends(j):
        image = multiply(j, [slice(0, 2), slice(6, 8)])
        acc[0:2] += image[0:2]
        acc[6:8] += image[2:4]

    def slot_of(block):
        source = block // 2
        across = jnp.where(col == source % 2, 0, 2) + jnp.where(row == source // 2, 0, 4)
        return across + block % 2

    def place(i):
        return jnp.where(2 * floor >= m, i, m - 1 - i)

    def record(u, j, act):
        act(pltpu.make_async_remote_copy(
            src_ref=sums.at[u, j], dst_ref=part.at[me, j], send_sem=sent.at[1], recv_sem=red_in.at[j],
            device_id={"tm": jnp.minimum(2 * chip + u, n - 1)}, device_id_type=MESH,
        ))

    def records(places, act, add, here=True):
        def one(i, _):
            j = place(i)
            mine_at = pl.ds(pl.multiple_of(j * share_size, share_size), share_size)
            there = pl.ds(pl.multiple_of(sensors + j * share_size, share_size), share_size)
            for u in places:
                @pl.when((2 * chip + u < n) & here)
                def _(u=u):
                    if add:
                        value = acc[slot_of(u), :, mine_at]
                        if u > 0:
                            value = value + acc[slot_of(u - 1), :, there]
                        sums[u, j] = value
                    if u > 1:
                        record(u, j, act)
                    else:
                        @pl.when(core != u)
                        def _():
                            record(u, j, act)

            return 0

        lax.fori_loop(0, m, one, 0)

    final = chunks - 1

    @pl.when(jnp.logical_not(inner))
    def _():
        arrive(0)
        arrive(1)
        for j in range(final):
            if j > 1:
                arrive(j)
            ready(j)
            taken(3, j, 2)
            compute(j, 0, n, j == 0)
        ready(final)
        taken(3, final, 2)
        pl.semaphore_wait(hello.at[1], greeted)

        @pl.when(first)
        def _():
            compute_ends(final)
            records((n - 1,), start, True)
            arrive(final)
            compute(final, 2, 6, False)
            records((6, 5, 3, 4, 2), start, True)

        @pl.when(jnp.logical_not(first))
        def _():
            compute(final, 0, n, False)

        records((1, 0), start, True)

    @pl.when(inner)
    def _():
        for j in range(chunks):
            arrive(j)
            ready(j)
            compute(j, 0, 6, j == 0)
        pl.semaphore_wait(hello.at[1], greeted)
        records((3, 2), start, True, chip == 1)
        records((1, 0), start, True)
        for j in [*range(split, chunks), *range(split)]:
            taken(3, j, 2)
            compute(j, 6, 8, j == split)
        records((3, 2), start, True, chip == 2)
        records((5, 4), start, True)

    for j in range(chunks):
        send_x(j, wait_send)
        send_y(j, wait_send)
        from_x(j, True, False, wait_send)
        from_y(j, True, False, wait_send)
    send_pair(wait_send)
    for p in (0, 1):
        swap(p, wait_send)

    def to_floor(other, act):
        act(pltpu.make_async_remote_copy(
            src_ref=total.at[other], dst_ref=share.at[floor],
            send_sem=sent.at[2], recv_sem=floor_in.at[0],
            device_id={"floor": other}, device_id_type=MESH,
        ))

    def gather_share(i, _):
        j = place(i)

        for c in range(chips):
            @pl.when(chip == c)
            def _(c=c):
                pltpu.make_async_remote_copy(
                    src_ref=sums.at[0:2 * c + 1, j], dst_ref=part.at[0:2 * c + 1, j], send_sem=sent.at[1],
                    recv_sem=red_in.at[j], device_id={"tm": pair}, device_id_type=MESH,
                ).wait_recv()

        def add_part(p, value):
            return value + part[jnp.where(p == 0, pair, 2 * chip - p), j]

        total[j] = lax.fori_loop(0, 2 * chip + 1, add_part, sums[core, j])

        @pl.when(j != floor)
        def _():
            to_floor(j, start)

        return 0

    lax.fori_loop(0, m, gather_share, 0)
    records(range(n - 1, -1, -1), wait_send, False)
    for step in range(1, m):
        to_floor(lax.rem(floor + step, m), wait_send)
    everyone = pl.ds(0, m - 1)
    pltpu.make_async_remote_copy(
        src_ref=total.at[everyone], dst_ref=share.at[everyone], send_sem=sent.at[2], recv_sem=floor_in.at[0],
        device_id={"floor": lax.rem(floor + 1, m)}, device_id_type=MESH,
    ).wait_recv()
    result = total[floor]
    for step in range(1, m):
        result = result + share[lax.rem(floor + step, m)]
    out_ref[0] = result.astype(out_ref.dtype)


def square_call(n, m, samples, operator):
    _, k, depth = samples.shape
    sensors = operator.shape[1]
    half = depth // 2
    widths = [part * half // 16 for part in (6, 6, 2, 2)]
    chunks = len(widths)
    dma = pltpu.SemaphoreType.DMA
    return pl.pallas_call(
        functools.partial(square, m, widths, 1),
        out_shape=pltpu.VMEM((1, k, sensors // m), jnp.bfloat16),
        in_specs=[pl.BlockSpec(memory_space=pl.ANY)] * 2,
        out_specs=pl.BlockSpec(memory_space=pltpu.VMEM),
        scratch_shapes=[
            pltpu.VMEM((n, k, half), jnp.bfloat16),
            pltpu.VMEM((k, depth), jnp.bfloat16),
            pltpu.VMEM((2, sensors, half), jnp.bfloat16),
            pltpu.VMEM((n, k, 2 * sensors), jnp.float32),
            pltpu.VMEM((n, m, k, sensors // m), jnp.float32),
            pltpu.VMEM((n, m, k, sensors // m), jnp.float32),
            pltpu.VMEM((m, k, sensors // m), jnp.float32),
            pltpu.VMEM((m, k, sensors // m), jnp.float32),
            dma((3,)), dma((2,)), dma((1,)), dma((4, chunks)), dma((3,)), dma((m,)), dma((1,)),
            pltpu.SemaphoreType.REGULAR((3,)),
        ],
        compiler_params=pltpu.CompilerParams(collective_id=0, has_side_effects=True),
    )(samples, operator)


def solution(mesh):
    n, m = mesh.shape["tm"], mesh.shape["floor"]

    def local(samples, operator):
        if grid_of(n // 2) == (2, 2):
            return square_call(n, m, samples, operator)
        _, k, depth = samples.shape
        sensors = operator.shape[1]
        chunks = 4
        width = depth // chunks
        return pl.pallas_call(
            functools.partial(kernel, n, m, chunks),
            out_shape=pltpu.VMEM((1, k, sensors // m), jnp.bfloat16),
            in_specs=[pl.BlockSpec(memory_space=pl.ANY)] * 2,
            out_specs=pl.BlockSpec(memory_space=pltpu.VMEM),
            scratch_shapes=[
                pltpu.VMEM((chunks, n, k, width), jnp.bfloat16),
                pltpu.VMEM((chunks, n, k, width), jnp.bfloat16),
                pltpu.VMEM((chunks, sensors, width), jnp.bfloat16),
                pltpu.VMEM((n, k, sensors), jnp.float32),
                pltpu.VMEM((n, k, sensors), jnp.float32),
                pltpu.VMEM((m, k, sensors // m), jnp.float32),
                pltpu.VMEM((m, k, sensors // m), jnp.float32),
                pltpu.SemaphoreType.DMA((chunks,)),
                pltpu.SemaphoreType.DMA((chunks,)),
                pltpu.SemaphoreType.DMA((chunks, n // 2)),
                pltpu.SemaphoreType.DMA((chunks,)),
                pltpu.SemaphoreType.DMA((chunks, n // 2)),
                pltpu.SemaphoreType.DMA((chunks, n // 2, max(1, max(grid_of(n // 2)) - 1))),
                pltpu.SemaphoreType.DMA((chunks, n)),
                pltpu.SemaphoreType.DMA((n,)),
                pltpu.SemaphoreType.DMA((n,)),
                pltpu.SemaphoreType.DMA((m,)),
                pltpu.SemaphoreType.DMA((m,)),
            ],
            compiler_params=pltpu.CompilerParams(collective_id=0, has_side_effects=True),
        )(samples, operator)

    placed = (P("tm", None, "floor"), P("tm", None, "floor"))
    return jax.shard_map(
        local, mesh=mesh, in_specs=placed, out_specs=P("tm", None, "floor"), check_vma=False
    )
```

```python
import functools

import jax
import jax.numpy as jnp
from jax import lax
from jax.experimental import pallas as pl
from jax.experimental.pallas import tpu as pltpu
from jax.sharding import PartitionSpec as P

MESH = pl.DeviceIdType.MESH
LOOK = 1


def each(low, high, body):
    if high - low <= 4:
        for i in range(low, high):
            body(i)
    else:
        def step(i, carry):
            body(i)
            return carry

        lax.fori_loop(low, high, step, 0)


def grid_of(chips):
    rows = 1
    while rows * rows * 4 <= chips and chips % (rows * 2) == 0:
        rows *= 2
    return rows, chips // rows


def kernel(
    n, m, chunks, x_hbm, op_hbm, out_ref, x, far, op, acc, part, total, share,
    own_sem, op_sem, out_sem, pair_sem, fwd_sem, relay_sem, in_sem,
    red_out, red_in, floor_out, floor_in,
):
    me, floor = lax.axis_index("tm"), lax.axis_index("floor")
    chips = n // 2
    rows, cols = grid_of(chips)
    chip, core = lax.div(me, 2), lax.rem(me, 2)
    row, col = lax.div(chip, cols), lax.rem(chip, cols)
    pair = 2 * chip + 1 - core
    k, width = x.shape[2], x.shape[3]
    sensors = op.shape[1]
    share_size = sensors // m

    def columns(c):
        return pl.ds(c * width, width)

    own = [pltpu.make_async_copy(x_hbm.at[0, :, columns(c)], x.at[c, me], own_sem.at[c]) for c in range(chunks)]
    weights = [pltpu.make_async_copy(op_hbm.at[0, :, columns(c)], op.at[c], op_sem.at[c]) for c in range(chunks)]
    for c in range(chunks):
        own[c].start()
        weights[c].start()

    barrier = pltpu.get_barrier_semaphore()
    for step in range(1, n):
        pl.semaphore_signal(barrier, inc=1, device_id={"tm": lax.rem(me + step, n)}, device_id_type=MESH)
    for step in range(1, m):
        pl.semaphore_signal(barrier, inc=1, device_id={"floor": lax.rem(floor + step, m)}, device_id_type=MESH)
    pl.semaphore_wait(barrier, n + m - 2)

    def need(block, at_chip):
        return 2 * at_chip + block < n

    many = max(rows, cols)

    def straight(source, at):
        return (lax.div(source, cols) == lax.div(at, cols)) | (lax.rem(source, cols) == lax.rem(at, cols))

    def relayed(odd, source, block, at, step):
        turn = lax.rem(core + odd, 2) == 0
        r, q = lax.div(source, cols), lax.rem(source, cols)
        r_at, q_at = lax.div(at, cols), lax.rem(at, cols)
        r_to, q_to = lax.rem(r + step, rows), lax.rem(q + step, cols)
        down = (r_at == r) & (step < rows) & (turn | ((r_to == 0) & (q == 0)))
        along = (q_at == q) & (step < cols) & (jnp.logical_not(turn) | ((q_to == 0) & (r == 0)))
        target = jnp.where(r_at == r, r_to * cols + q_at, r_at * cols + q_to)
        return (at != 0) & (down | along) & need(block, target), 2 * target + core

    def route(odd, source, block, at):
        passes = at < 0
        for step in range(1, many):
            passes = passes | relayed(odd, source, block, at, step)[0]
        return straight(source, at) & (need(block, at) | passes), passes

    def make_plan(step, odd):
        other = lax.rem(chip + step, chips)
        block = 2 * other + core
        wanted, _ = route(odd, chip, me, other)
        _, passes = route(odd, other, block, chip)
        near = straight(other, chip)
        here = need(block, chip) & near, need(block, chip) & jnp.logical_not(near)
        alone = here[0] & jnp.logical_not(passes)
        onward = [relayed(odd, other, block, chip, s) for s in range(1, many)]
        return other, block, wanted, passes, here, alone, onward

    plans = {}
    if chips <= 5:
        plans = {(step, odd): make_plan(step, odd) for step in range(1, chips) for odd in (0, 1)}

    def plan(step, c):
        return plans[step, c % 2] if plans else make_plan(step, c % 2)

    others = [2 * lax.rem(chip + step, chips) + 1 - core for step in range(chips)] if plans else None
    def other_here(block):
        near = straight(lax.div(block, 2), chip)
        return need(block, chip) & near, need(block, chip) & jnp.logical_not(near)

    others_here = [other_here(block) for block in others] if plans else None
    self_here = need(me, chip)

    busy = need(2 * row * cols, chip) | need(2 * col, chip)

    def send(c, block, target, sem, source=None, into=None):
        return pltpu.make_async_remote_copy(
            src_ref=x.at[c, block] if source is None else source,
            dst_ref=(x if into is None else into).at[c, block],
            send_sem=sem, recv_sem=in_sem.at[c, block], device_id={"tm": target}, device_id_type=MESH,
        )

    def mine(c):
        return x_hbm.at[0, :, columns(c)]

    def sends(c, act):
        def one(step):
            _, block, wanted, *_ = plan(step, c)

            @pl.when(wanted)
            def _():
                act(send(c, me, block, out_sem.at[c, step], mine(c)))

        each(1, chips, one)

        @pl.when(self_here)
        def _():
            act(send(c, me, pair, pair_sem.at[c], mine(c)))

    def relays(c, act, wait):
        def one(step):
            source, block, _, passes, _, _, onward = plan(step, c)

            @pl.when(passes)
            def _():
                if wait:
                    send(c, block, pair, fwd_sem.at[c, source]).wait_recv()
                for s, (wanted, target) in enumerate(onward):
                    @pl.when(wanted)
                    def _(s=s, target=target):
                        act(send(c, block, target, relay_sem.at[c, source, s], None, far))

        each(1, chips, one)

    def forwards(c, act, wait):
        def one(step):
            source, block, _, _, here, alone, _ = plan(step, c)
            if wait:
                @pl.when(alone)
                def _():
                    send(c, block, pair, fwd_sem.at[c, source]).wait_recv()

            @pl.when(here[0])
            def _():
                act(send(c, block, pair, fwd_sem.at[c, source]))

        each(1, chips, one)

    def far_forwards(c, act, wait):
        def one(step):
            source, block, _, _, here, _, _ = plan(step, c)

            @pl.when(here[1])
            def _():
                copy = send(c, block, pair, fwd_sem.at[c, source], far.at[c, block], far)
                if wait:
                    copy.wait_recv()
                act(copy)

        each(1, chips, one)

    def take(c, part_of):
        def one(step):
            block = others[step] if plans else 2 * lax.rem(chip + step, chips) + 1 - core
            here = (others_here[step] if plans else other_here(block))[part_of]

            @pl.when(here)
            def _():
                send(c, block, pair, pair_sem.at[c], None, far if part_of else None).wait_recv()

        each(0, chips, one)

    def start(copy):
        copy.start()

    def wait_send(copy):
        copy.wait_send()


    tile = min(n, max(1, 128 // k))

    def image_of(block_rows, c):
        return lax.dot_general(
            block_rows.reshape(-1, width), op[c], (((1,), (1,)), ((), ())), preferred_element_type=jnp.float32
        ).reshape(-1, k, sensors)

    for c in range(chunks):
        sends(c, start)
    for c in range(min(LOOK, chunks)):
        relays(c, start, True)
    forwards(0, start, True)
    for c in range(chunks):
        if c + LOOK < chunks:
            relays(c + LOOK, start, True)
        if c + 1 < chunks:
            forwards(c + 1, start, True)
        take(c, 0)
        own[c].wait()
        weights[c].wait()

        @pl.when(busy)
        def _(c=c):
            for r in range(n // tile):
                image = image_of(x[c, r * tile:(r + 1) * tile], c)
                if c == 0:
                    acc[r * tile:(r + 1) * tile] = image
                else:
                    acc[r * tile:(r + 1) * tile] += image

    def lag_part(step):
        return pltpu.make_async_remote_copy(
            src_ref=acc.at[step], dst_ref=part.at[me],
            send_sem=red_out.at[step], recv_sem=red_in.at[me],
            device_id={"tm": lax.rem(me + step, n)}, device_id_type=MESH,
        )

    def lag_parts(near, act):
        for step in range(n - 1, 0, -1):
            @pl.when((me + step < n) & (straight(step // 2, chip) == near))
            def _(step=step):
                act(lag_part(step))

    lag_parts(True, start)

    far_forwards(0, start, True)
    for c in range(chunks):
        if c + 1 < chunks:
            far_forwards(c + 1, start, True)
        take(c, 1)

        def far_images(step, c=c):
            r = lax.rem(row + 1 + lax.div(step, max(1, cols - 1)), rows)
            q = lax.rem(col + 1 + lax.rem(step, max(1, cols - 1)), cols)
            source = r * cols + q

            @pl.when(need(2 * source, chip))
            def _():
                image = image_of(far[c, pl.ds(2 * source, 2)], c)
                if c == 0:
                    acc[pl.ds(2 * source, 2)] = image
                else:
                    acc[pl.ds(2 * source, 2)] += image

        each(0, (rows - 1) * (cols - 1), far_images)

    lag_parts(False, start)

    for c in range(chunks):
        sends(c, wait_send)
        relays(c, wait_send, False)
        forwards(c, wait_send, False)
        far_forwards(c, wait_send, False)

    def add_lag(lag, value):
        pltpu.make_async_remote_copy(
            src_ref=acc.at[0], dst_ref=part.at[lag],
            send_sem=red_out.at[0], recv_sem=red_in.at[lag],
            device_id={"tm": pair}, device_id_type=MESH,
        ).wait_recv()
        return value + part[lag]

    value = lax.fori_loop(0, me, add_lag, acc[0])
    for j in range(m):
        total[j] = value[:, j * share_size:(j + 1) * share_size]

    def to_floor(step):
        other = lax.rem(floor + step, m)
        return pltpu.make_async_remote_copy(
            src_ref=total.at[other], dst_ref=share.at[floor],
            send_sem=floor_out.at[step], recv_sem=floor_in.at[floor],
            device_id={"floor": other}, device_id_type=MESH,
        )

    for step in range(m - 1, 0, -1):
        to_floor(step).start()
    result = total[floor]
    for step in range(1, m):
        source = lax.rem(floor + step, m)
        pltpu.make_async_remote_copy(
            src_ref=total.at[source], dst_ref=share.at[source],
            send_sem=floor_out.at[step], recv_sem=floor_in.at[source],
            device_id={"floor": source}, device_id_type=MESH,
        ).wait_recv()
        result = result + share[source]
    out_ref[0] = result.astype(out_ref.dtype)

    lag_parts(True, wait_send)
    lag_parts(False, wait_send)
    for step in range(1, m):
        to_floor(step).wait_send()


def square(
    m, widths, split, x_hbm, op_hbm, out_ref, x, mine, op, acc, sums, part, total, share,
    load_sem, swap_in, pair_in, in_sem, sent, red_in, floor_in, hello,
):
    n = part.shape[0]
    chips = n // 2
    me, floor = lax.axis_index("tm"), lax.axis_index("floor")
    chip, core = lax.div(me, 2), lax.rem(me, 2)
    row, col = lax.div(chip, 2), lax.rem(chip, 2)
    sources = [chip, 2 * row + 1 - col, 2 * (1 - row) + col, 2 * (1 - row) + 1 - col]
    other = 1 - core
    pair = 2 * chip + other
    chunks, starts = len(widths), [sum(widths[:j]) for j in range(len(widths))]
    k, depth = x.shape[1], x.shape[2]
    sensors = op.shape[1]
    share_size = sensors // m
    inner = (chip == 1) | (chip == 2)

    def columns(half, j):
        begin, size = (starts[j], widths[j]) if isinstance(j, int) else (j * widths[0], widths[0])
        return pl.ds(pl.multiple_of(half * depth + begin, 128), size)

    def at(j):
        if isinstance(j, int):
            return slice(starts[j], starts[j] + widths[j])
        return pl.ds(pl.multiple_of(j * widths[0], 128), widths[0])

    own = pltpu.make_async_copy(x_hbm.at[0, :, pl.ds(pl.multiple_of(core * depth, 128), depth)], x.at[core], load_sem.at[0])
    staged = pltpu.make_async_copy(x_hbm.at[0], mine, load_sem.at[1])
    weights = pltpu.make_async_copy(
        op_hbm.at[0, :, pl.ds(pl.multiple_of(core * depth, 128), depth)], op.at[core], load_sem.at[2]
    )
    staged.start()
    own.start()

    neighbours = (2 * sources[1], 2 * sources[1] + 1, 2 * sources[2], 2 * sources[2] + 1)

    def to_upper(sem):
        @pl.when(floor < m - 1)
        def _():
            pl.semaphore_signal(sem, inc=1, device_id={"floor": jnp.minimum(floor + 1, m - 1)}, device_id_type=MESH)

    def to_lower(sem):
        @pl.when(floor > 0)
        def _():
            pl.semaphore_signal(sem, inc=1, device_id={"floor": jnp.maximum(floor - 1, 0)}, device_id_type=MESH)

    def in_plane(sem, all_round):
        pl.semaphore_signal(sem, inc=1, device_id={"tm": pair}, device_id_type=MESH)

        @pl.when(all_round)
        def _():
            for target in neighbours:
                pl.semaphore_signal(sem, inc=1, device_id={"tm": target}, device_id_type=MESH)

    def greet(sem):
        in_plane(sem, True)
        to_upper(sem)
        to_lower(sem)

    below, above = jnp.where(floor > 0, 1, 0), jnp.where(floor < m - 1, 1, 0)
    greeted = 5 + below + above
    barrier = pltpu.get_barrier_semaphore()
    in_plane(barrier, chip < chips - 1)
    to_upper(barrier)
    pl.semaphore_wait(barrier, jnp.where(inner, 3, 5) + below)

    @pl.when(chip == chips - 1)
    def _():
        for target in neighbours:
            pl.semaphore_signal(hello.at[2], inc=1, device_id={"tm": target}, device_id_type=MESH)

    to_lower(hello.at[3])

    def need(source, at):
        return source + at < chips

    needs = [need(source, chip) for source in sources]

    def by_x(source, parity, j):
        outer = (source == 0) | (source == chips - 1)
        through_first = jnp.where(source == 1, j < split, j >= split)
        return (outer & (parity == j % 2)) | (jnp.logical_not(outer) & through_first)

    def remote(src, dst, out, into, target):
        return pltpu.make_async_remote_copy(
            src_ref=src, dst_ref=dst, send_sem=out, recv_sem=into, device_id={"tm": target}, device_id_type=MESH
        )

    def start(copy):
        copy.start()

    def wait_send(copy):
        copy.wait_send()

    def send_x(j, act):
        @pl.when(needs_at_x | by_x(chip, core, j))
        def _():
            for half in (0, 1):
                act(remote(mine.at[:, columns(half, j)], x.at[2 + core, :, at(j)], sent.at[0], in_sem.at[0, j], 2 * sources[1] + half))

    def send_y(j, act):
        @pl.when(needs_at_y | jnp.logical_not(by_x(chip, core, j)))
        def _():
            for half in (0, 1):
                act(remote(mine.at[:, columns(half, j)], x.at[4 + core, :, at(j)], sent.at[0], in_sem.at[1, j], 2 * sources[2] + half))

    needs_at_x, needs_at_y = need(chip, sources[1]), need(chip, sources[2])

    def send_pair(act):
        there = pl.ds(pl.multiple_of(other * depth, 128), depth)
        act(remote(mine.at[:, there], x.at[core], sent.at[0], pair_in.at[0], pair))

    parts = (slice(0, starts[2]), slice(starts[2], depth))

    def swap(p, act):
        begin, size = parts[p].start, parts[p].stop - parts[p].start
        there = pl.ds(pl.multiple_of(other * depth + begin, 128), size)
        act(remote(op_hbm.at[0, :, there], op.at[core, :, parts[p]], sent.at[0], swap_in.at[p], pair))

    def swapped(p):
        remote(op.at[core, :, parts[p]], op.at[other, :, parts[p]], sent.at[0], swap_in.at[p], pair).wait_recv()

    def taken(source, j, blocks):
        here = x.at[2 * source:2 * source + blocks, :, at(j)]
        remote(here, here, sent.at[0], in_sem.at[source - 1, j], pair).wait_recv()

    def pass_x(j, parity, act):
        act(remote(x.at[2 + parity, :, at(j)], x.at[6 + parity, :, at(j)], sent.at[0], in_sem.at[2, j], 2 * sources[2] + core))

    def pass_y(j, parity, act):
        act(remote(x.at[4 + parity, :, at(j)], x.at[6 + parity, :, at(j)], sent.at[0], in_sem.at[2, j], 2 * sources[1] + core))

    def come(source, j, both, onward):
        count = onward[0].astype(jnp.int32) + onward[1].astype(jnp.int32)
        for blocks in (1, 2):
            @pl.when(jnp.where(both, 2, count) == blocks)
            def _(blocks=blocks):
                taken(source, j, blocks)

    def from_x(j, here, wait, act):
        onward = [by_x(sources[1], parity, j) for parity in (0, 1)]

        @pl.when(here)
        def _():
            if wait:
                come(1, j, needs[1], onward)
            for parity in (0, 1):
                @pl.when(onward[parity])
                def _(parity=parity):
                    pass_x(j, parity, act)

    def from_y(j, here, wait, act):
        onward = [jnp.logical_not(by_x(sources[2], parity, j)) for parity in (0, 1)]

        @pl.when(here)
        def _():
            if wait:
                come(2, j, needs[2], onward)
            for parity in (0, 1):
                @pl.when(onward[parity])
                def _(parity=parity):
                    pass_y(j, parity, act)

    lead = chunks // 2
    staged.wait()
    for j in range(chunks):
        at_once = jnp.logical_not(inner) | (j < lead)

        @pl.when(at_once & needs_at_x)
        def _(j=j):
            send_x(j, start)

        @pl.when(at_once & needs_at_y)
        def _(j=j):
            send_y(j, start)

    across = [*range(lead, chunks), *range(split, lead), *range(split)]

    def send_only_across(turns):
        for j in turns:
            @pl.when(jnp.logical_not(needs_at_x))
            def _(j=j):
                send_x(j, start)

            @pl.when(jnp.logical_not(needs_at_y))
            def _(j=j):
                send_y(j, start)

    @pl.when(chip == chips - 1)
    def _():
        send_only_across(range(chunks))

    weights.start()
    send_pair(start)
    for p in (0, 1):
        swap(p, start)

    @pl.when(inner)
    def _():
        pl.semaphore_wait(hello.at[2], 2)
        send_only_across(across)

    @pl.when(floor < m - 1)
    def _():
        pl.semaphore_wait(hello.at[3], 1)

    greet(hello.at[0])

    def send_late(j):
        @pl.when(needs_at_x)
        def _():
            send_x(j, start)

        @pl.when(needs_at_y)
        def _():
            send_y(j, start)

    def passing(j):
        from_x(j, jnp.logical_not(needs[1]), True, start)
        from_y(j, jnp.logical_not(needs[2]), True, start)

    @pl.when(inner)
    def _():
        for j in range(chunks):
            passing(j)
            for late in range(lead, chunks):
                if j == min(2 * (late - lead) + 1, chunks - 1):
                    send_late(late)

    @pl.when(chip == chips - 1)
    def _():
        for j in across:
            passing(j)

    pl.semaphore_wait(hello.at[0], greeted)
    greet(hello.at[1])

    def arrive(j):
        from_x(j, needs[1], True, start)
        from_y(j, needs[2], True, start)
    first = chip == 0

    def ready(j):
        if j == 0:
            own.wait()
            weights.wait()
            remote(x.at[other], x.at[other], sent.at[0], pair_in.at[0], pair).wait_recv()
            swapped(0)
        if j == 2:
            swapped(1)

    def multiply(j, pieces):
        rows = jnp.concatenate([x[p, :, at(j)] for p in pieces], axis=0)
        depth_here = rows.shape[-1]
        return lax.dot_general(
            rows.reshape(-1, depth_here), op[:, :, at(j)].reshape(-1, depth_here), (((1,), (1,)), ((), ())),
            preferred_element_type=jnp.float32,
        ).reshape(-1, k, 2 * sensors)

    def compute(j, low, high, begin):
        image = multiply(j, [slice(low, high)])
        if begin:
            acc[low:high] = image
        else:
            acc[low:high] += image

    def compute_ends(j):
        image = multiply(j, [slice(0, 2), slice(6, 8)])
        acc[0:2] += image[0:2]
        acc[6:8] += image[2:4]

    def slot_of(block):
        source = block // 2
        across = jnp.where(col == source % 2, 0, 2) + jnp.where(row == source // 2, 0, 4)
        return across + block % 2

    def place(i):
        return jnp.where(i == m - 1, floor, jnp.where(i < floor, i, i + 1))

    def record(u, j, act):
        act(pltpu.make_async_remote_copy(
            src_ref=sums.at[u, j], dst_ref=part.at[me, j], send_sem=sent.at[1], recv_sem=red_in.at[j],
            device_id={"tm": jnp.minimum(2 * chip + u, n - 1)}, device_id_type=MESH,
        ))

    def records(places, act, add, here=True, low=0, high=m):
        def one(i, _):
            j = place(i)
            mine_at = pl.ds(pl.multiple_of(j * share_size, share_size), share_size)
            there = pl.ds(pl.multiple_of(sensors + j * share_size, share_size), share_size)
            for u in places:
                @pl.when((2 * chip + u < n) & here)
                def _(u=u):
                    if add:
                        sums[u, j] = acc[slot_of(u), :, mine_at] + acc[slot_of(u - 1), :, there]
                    record(u, j, act)

            return 0

        lax.fori_loop(low, high, one, 0)

    def swap_records(act):
        act(remote(sums.at[other], part.at[2 * chip], sent.at[1], pair_in.at[1], pair))

    def own_records():
        for j in range(m):
            mine_at = slice(j * share_size, (j + 1) * share_size)
            there = slice(sensors + j * share_size, sensors + (j + 1) * share_size)
            sums[0, j] = acc[slot_of(0), :, mine_at]
            sums[1, j] = acc[slot_of(1), :, mine_at] + acc[slot_of(0), :, there]
        swap_records(start)

    final = chunks - 1

    @pl.when(jnp.logical_not(inner))
    def _():
        arrive(0)
        arrive(1)
        for j in range(final):
            if j > 1:
                arrive(j)
            ready(j)
            taken(3, j, 2)
            compute(j, 0, n, j == 0)
        ready(final)
        taken(3, final, 2)
        pl.semaphore_wait(hello.at[1], greeted)

        @pl.when(first)
        def _():
            compute_ends(final)
            records((n - 1,), start, True, True, 0, 1)
            own_records()
            arrive(final)
            compute(final, 2, 6, False)
            records((6, 3, 2, 5, 4), start, True, True, 0, 1)
            records((6, 3, 2, 5, 4, n - 1), start, True, True, 1, m)

        @pl.when(jnp.logical_not(first))
        def _():
            compute(final, 0, n, False)
            own_records()

    @pl.when(inner)
    def _():
        for j in range(chunks):
            arrive(j)
            ready(j)
            compute(j, 0, 6, j == 0)
        pl.semaphore_wait(hello.at[1], greeted)
        records((3, 2), start, True, chip == 1)
        own_records()
        for j in across:
            taken(3, j, 2)
            compute(j, 6, 8, j == across[0])
        records((3, 2), start, True, chip == 2)
        records((5, 4), start, True)

    for j in range(chunks):
        send_x(j, wait_send)
        send_y(j, wait_send)
        from_x(j, True, False, wait_send)
        from_y(j, True, False, wait_send)
    send_pair(wait_send)
    for p in (0, 1):
        swap(p, wait_send)

    def to_floor(other, act):
        act(pltpu.make_async_remote_copy(
            src_ref=total.at[other], dst_ref=share.at[floor],
            send_sem=sent.at[2], recv_sem=floor_in.at[0],
            device_id={"floor": other}, device_id_type=MESH,
        ))

    def gather_share(i, _):
        j = place(i)

        for c in range(1, chips):
            @pl.when(chip == c)
            def _(c=c):
                pltpu.make_async_remote_copy(
                    src_ref=sums.at[0:2 * c, j], dst_ref=part.at[0:2 * c, j], send_sem=sent.at[1],
                    recv_sem=red_in.at[j], device_id={"tm": pair}, device_id_type=MESH,
                ).wait_recv()

        def add_part(p, value):
            return value + part[p, j]

        total[j] = lax.fori_loop(0, 2 * chip, add_part, sums[core, j] + part[2 * chip, j])

        @pl.when(j != floor)
        def _():
            to_floor(j, start)

        return 0

    remote(sums.at[0], part.at[2 * chip], sent.at[1], pair_in.at[1], pair).wait_recv()
    lax.fori_loop(0, m, gather_share, 0)
    records(range(n - 1, 1, -1), wait_send, False)
    swap_records(wait_send)
    for step in range(1, m):
        to_floor(lax.rem(floor + step, m), wait_send)
    everyone = pl.ds(0, m - 1)
    pltpu.make_async_remote_copy(
        src_ref=total.at[everyone], dst_ref=share.at[everyone], send_sem=sent.at[2], recv_sem=floor_in.at[0],
        device_id={"floor": lax.rem(floor + 1, m)}, device_id_type=MESH,
    ).wait_recv()
    result = total[floor]
    for step in range(1, m):
        result = result + share[lax.rem(floor + step, m)]
    out_ref[0] = result.astype(out_ref.dtype)


def square_call(n, m, samples, operator):
    _, k, depth = samples.shape
    sensors = operator.shape[1]
    half = depth // 2
    widths = [part * half // 16 for part in (7, 5, 2, 2)]
    chunks = len(widths)
    dma = pltpu.SemaphoreType.DMA
    return pl.pallas_call(
        functools.partial(square, m, widths, 1),
        out_shape=pltpu.VMEM((1, k, sensors // m), jnp.bfloat16),
        in_specs=[pl.BlockSpec(memory_space=pl.ANY)] * 2,
        out_specs=pl.BlockSpec(memory_space=pltpu.VMEM),
        scratch_shapes=[
            pltpu.VMEM((n, k, half), jnp.bfloat16),
            pltpu.VMEM((k, depth), jnp.bfloat16),
            pltpu.VMEM((2, sensors, half), jnp.bfloat16),
            pltpu.VMEM((n, k, 2 * sensors), jnp.float32),
            pltpu.VMEM((n, m, k, sensors // m), jnp.float32),
            pltpu.VMEM((n, m, k, sensors // m), jnp.float32),
            pltpu.VMEM((m, k, sensors // m), jnp.float32),
            pltpu.VMEM((m, k, sensors // m), jnp.float32),
            dma((3,)), dma((2,)), dma((2,)), dma((3, chunks)), dma((3,)), dma((m,)), dma((1,)),
            pltpu.SemaphoreType.REGULAR((4,)),
        ],
        compiler_params=pltpu.CompilerParams(collective_id=0, has_side_effects=True),
    )(samples, operator)


def solution(mesh):
    n, m = mesh.shape["tm"], mesh.shape["floor"]

    def local(samples, operator):
        if grid_of(n // 2) == (2, 2):
            return square_call(n, m, samples, operator)
        _, k, depth = samples.shape
        sensors = operator.shape[1]
        chunks = 4
        width = depth // chunks
        return pl.pallas_call(
            functools.partial(kernel, n, m, chunks),
            out_shape=pltpu.VMEM((1, k, sensors // m), jnp.bfloat16),
            in_specs=[pl.BlockSpec(memory_space=pl.ANY)] * 2,
            out_specs=pl.BlockSpec(memory_space=pltpu.VMEM),
            scratch_shapes=[
                pltpu.VMEM((chunks, n, k, width), jnp.bfloat16),
                pltpu.VMEM((chunks, n, k, width), jnp.bfloat16),
                pltpu.VMEM((chunks, sensors, width), jnp.bfloat16),
                pltpu.VMEM((n, k, sensors), jnp.float32),
                pltpu.VMEM((n, k, sensors), jnp.float32),
                pltpu.VMEM((m, k, sensors // m), jnp.float32),
                pltpu.VMEM((m, k, sensors // m), jnp.float32),
                pltpu.SemaphoreType.DMA((chunks,)),
                pltpu.SemaphoreType.DMA((chunks,)),
                pltpu.SemaphoreType.DMA((chunks, n // 2)),
                pltpu.SemaphoreType.DMA((chunks,)),
                pltpu.SemaphoreType.DMA((chunks, n // 2)),
                pltpu.SemaphoreType.DMA((chunks, n // 2, max(1, max(grid_of(n // 2)) - 1))),
                pltpu.SemaphoreType.DMA((chunks, n)),
                pltpu.SemaphoreType.DMA((n,)),
                pltpu.SemaphoreType.DMA((n,)),
                pltpu.SemaphoreType.DMA((m,)),
                pltpu.SemaphoreType.DMA((m,)),
            ],
            compiler_params=pltpu.CompilerParams(collective_id=0, has_side_effects=True),
        )(samples, operator)

    placed = (P("tm", None, "floor"), P("tm", None, "floor"))
    return jax.shard_map(
        local, mesh=mesh, in_specs=placed, out_specs=P("tm", None, "floor"), check_vma=False
    )
```

```python
import functools

import jax
import jax.numpy as jnp
from jax import lax
from jax.experimental import pallas as pl
from jax.experimental.pallas import tpu as pltpu
from jax.sharding import PartitionSpec as P

MESH = pl.DeviceIdType.MESH
LOOK = 1


def each(low, high, body):
    if high - low <= 4:
        for i in range(low, high):
            body(i)
    else:
        def step(i, carry):
            body(i)
            return carry

        lax.fori_loop(low, high, step, 0)


def grid_of(chips):
    rows = 1
    while rows * rows * 4 <= chips and chips % (rows * 2) == 0:
        rows *= 2
    return rows, chips // rows


def kernel(
    n, m, chunks, x_hbm, op_hbm, out_ref, x, far, op, acc, part, total, share,
    own_sem, op_sem, out_sem, pair_sem, fwd_sem, relay_sem, in_sem,
    red_out, red_in, floor_out, floor_in,
):
    me, floor = lax.axis_index("tm"), lax.axis_index("floor")
    chips = n // 2
    rows, cols = grid_of(chips)
    chip, core = lax.div(me, 2), lax.rem(me, 2)
    row, col = lax.div(chip, cols), lax.rem(chip, cols)
    pair = 2 * chip + 1 - core
    k, width = x.shape[2], x.shape[3]
    sensors = op.shape[1]
    share_size = sensors // m

    def columns(c):
        return pl.ds(c * width, width)

    own = [pltpu.make_async_copy(x_hbm.at[0, :, columns(c)], x.at[c, me], own_sem.at[c]) for c in range(chunks)]
    weights = [pltpu.make_async_copy(op_hbm.at[0, :, columns(c)], op.at[c], op_sem.at[c]) for c in range(chunks)]
    for c in range(chunks):
        own[c].start()
        weights[c].start()

    barrier = pltpu.get_barrier_semaphore()
    for step in range(1, n):
        pl.semaphore_signal(barrier, inc=1, device_id={"tm": lax.rem(me + step, n)}, device_id_type=MESH)
    for step in range(1, m):
        pl.semaphore_signal(barrier, inc=1, device_id={"floor": lax.rem(floor + step, m)}, device_id_type=MESH)
    pl.semaphore_wait(barrier, n + m - 2)

    def need(block, at_chip):
        return 2 * at_chip + block < n

    many = max(rows, cols)

    def straight(source, at):
        return (lax.div(source, cols) == lax.div(at, cols)) | (lax.rem(source, cols) == lax.rem(at, cols))

    def relayed(odd, source, block, at, step):
        turn = lax.rem(core + odd, 2) == 0
        r, q = lax.div(source, cols), lax.rem(source, cols)
        r_at, q_at = lax.div(at, cols), lax.rem(at, cols)
        r_to, q_to = lax.rem(r + step, rows), lax.rem(q + step, cols)
        down = (r_at == r) & (step < rows) & (turn | ((r_to == 0) & (q == 0)))
        along = (q_at == q) & (step < cols) & (jnp.logical_not(turn) | ((q_to == 0) & (r == 0)))
        target = jnp.where(r_at == r, r_to * cols + q_at, r_at * cols + q_to)
        return (at != 0) & (down | along) & need(block, target), 2 * target + core

    def route(odd, source, block, at):
        passes = at < 0
        for step in range(1, many):
            passes = passes | relayed(odd, source, block, at, step)[0]
        return straight(source, at) & (need(block, at) | passes), passes

    def make_plan(step, odd):
        other = lax.rem(chip + step, chips)
        block = 2 * other + core
        wanted, _ = route(odd, chip, me, other)
        _, passes = route(odd, other, block, chip)
        near = straight(other, chip)
        here = need(block, chip) & near, need(block, chip) & jnp.logical_not(near)
        alone = here[0] & jnp.logical_not(passes)
        onward = [relayed(odd, other, block, chip, s) for s in range(1, many)]
        return other, block, wanted, passes, here, alone, onward

    plans = {}
    if chips <= 5:
        plans = {(step, odd): make_plan(step, odd) for step in range(1, chips) for odd in (0, 1)}

    def plan(step, c):
        return plans[step, c % 2] if plans else make_plan(step, c % 2)

    others = [2 * lax.rem(chip + step, chips) + 1 - core for step in range(chips)] if plans else None
    def other_here(block):
        near = straight(lax.div(block, 2), chip)
        return need(block, chip) & near, need(block, chip) & jnp.logical_not(near)

    others_here = [other_here(block) for block in others] if plans else None
    self_here = need(me, chip)

    busy = need(2 * row * cols, chip) | need(2 * col, chip)

    def send(c, block, target, sem, source=None, into=None):
        return pltpu.make_async_remote_copy(
            src_ref=x.at[c, block] if source is None else source,
            dst_ref=(x if into is None else into).at[c, block],
            send_sem=sem, recv_sem=in_sem.at[c, block], device_id={"tm": target}, device_id_type=MESH,
        )

    def mine(c):
        return x_hbm.at[0, :, columns(c)]

    def sends(c, act):
        def one(step):
            _, block, wanted, *_ = plan(step, c)

            @pl.when(wanted)
            def _():
                act(send(c, me, block, out_sem.at[c, step], mine(c)))

        each(1, chips, one)

        @pl.when(self_here)
        def _():
            act(send(c, me, pair, pair_sem.at[c], mine(c)))

    def relays(c, act, wait):
        def one(step):
            source, block, _, passes, _, _, onward = plan(step, c)

            @pl.when(passes)
            def _():
                if wait:
                    send(c, block, pair, fwd_sem.at[c, source]).wait_recv()
                for s, (wanted, target) in enumerate(onward):
                    @pl.when(wanted)
                    def _(s=s, target=target):
                        act(send(c, block, target, relay_sem.at[c, source, s], None, far))

        each(1, chips, one)

    def forwards(c, act, wait):
        def one(step):
            source, block, _, _, here, alone, _ = plan(step, c)
            if wait:
                @pl.when(alone)
                def _():
                    send(c, block, pair, fwd_sem.at[c, source]).wait_recv()

            @pl.when(here[0])
            def _():
                act(send(c, block, pair, fwd_sem.at[c, source]))

        each(1, chips, one)

    def far_forwards(c, act, wait):
        def one(step):
            source, block, _, _, here, _, _ = plan(step, c)

            @pl.when(here[1])
            def _():
                copy = send(c, block, pair, fwd_sem.at[c, source], far.at[c, block], far)
                if wait:
                    copy.wait_recv()
                act(copy)

        each(1, chips, one)

    def take(c, part_of):
        def one(step):
            block = others[step] if plans else 2 * lax.rem(chip + step, chips) + 1 - core
            here = (others_here[step] if plans else other_here(block))[part_of]

            @pl.when(here)
            def _():
                send(c, block, pair, pair_sem.at[c], None, far if part_of else None).wait_recv()

        each(0, chips, one)

    def start(copy):
        copy.start()

    def wait_send(copy):
        copy.wait_send()


    tile = min(n, max(1, 128 // k))

    def image_of(block_rows, c):
        return lax.dot_general(
            block_rows.reshape(-1, width), op[c], (((1,), (1,)), ((), ())), preferred_element_type=jnp.float32
        ).reshape(-1, k, sensors)

    for c in range(chunks):
        sends(c, start)
    for c in range(min(LOOK, chunks)):
        relays(c, start, True)
    forwards(0, start, True)
    for c in range(chunks):
        if c + LOOK < chunks:
            relays(c + LOOK, start, True)
        if c + 1 < chunks:
            forwards(c + 1, start, True)
        take(c, 0)
        own[c].wait()
        weights[c].wait()

        @pl.when(busy)
        def _(c=c):
            for r in range(n // tile):
                image = image_of(x[c, r * tile:(r + 1) * tile], c)
                if c == 0:
                    acc[r * tile:(r + 1) * tile] = image
                else:
                    acc[r * tile:(r + 1) * tile] += image

    def lag_part(step):
        return pltpu.make_async_remote_copy(
            src_ref=acc.at[step], dst_ref=part.at[me],
            send_sem=red_out.at[step], recv_sem=red_in.at[me],
            device_id={"tm": lax.rem(me + step, n)}, device_id_type=MESH,
        )

    def lag_parts(near, act):
        for step in range(n - 1, 0, -1):
            @pl.when((me + step < n) & (straight(step // 2, chip) == near))
            def _(step=step):
                act(lag_part(step))

    lag_parts(True, start)

    far_forwards(0, start, True)
    for c in range(chunks):
        if c + 1 < chunks:
            far_forwards(c + 1, start, True)
        take(c, 1)

        def far_images(step, c=c):
            r = lax.rem(row + 1 + lax.div(step, max(1, cols - 1)), rows)
            q = lax.rem(col + 1 + lax.rem(step, max(1, cols - 1)), cols)
            source = r * cols + q

            @pl.when(need(2 * source, chip))
            def _():
                image = image_of(far[c, pl.ds(2 * source, 2)], c)
                if c == 0:
                    acc[pl.ds(2 * source, 2)] = image
                else:
                    acc[pl.ds(2 * source, 2)] += image

        each(0, (rows - 1) * (cols - 1), far_images)

    lag_parts(False, start)

    for c in range(chunks):
        sends(c, wait_send)
        relays(c, wait_send, False)
        forwards(c, wait_send, False)
        far_forwards(c, wait_send, False)

    def add_lag(lag, value):
        pltpu.make_async_remote_copy(
            src_ref=acc.at[0], dst_ref=part.at[lag],
            send_sem=red_out.at[0], recv_sem=red_in.at[lag],
            device_id={"tm": pair}, device_id_type=MESH,
        ).wait_recv()
        return value + part[lag]

    value = lax.fori_loop(0, me, add_lag, acc[0])
    for j in range(m):
        total[j] = value[:, j * share_size:(j + 1) * share_size]

    def to_floor(step):
        other = lax.rem(floor + step, m)
        return pltpu.make_async_remote_copy(
            src_ref=total.at[other], dst_ref=share.at[floor],
            send_sem=floor_out.at[step], recv_sem=floor_in.at[floor],
            device_id={"floor": other}, device_id_type=MESH,
        )

    for step in range(m - 1, 0, -1):
        to_floor(step).start()
    result = total[floor]
    for step in range(1, m):
        source = lax.rem(floor + step, m)
        pltpu.make_async_remote_copy(
            src_ref=total.at[source], dst_ref=share.at[source],
            send_sem=floor_out.at[step], recv_sem=floor_in.at[source],
            device_id={"floor": source}, device_id_type=MESH,
        ).wait_recv()
        result = result + share[source]
    out_ref[0] = result.astype(out_ref.dtype)

    lag_parts(True, wait_send)
    lag_parts(False, wait_send)
    for step in range(1, m):
        to_floor(step).wait_send()


def square(
    m, widths, through, x_hbm, op_hbm, out_ref, x, mine, op, acc, sums, part, total, share,
    load_sem, swap_in, pair_in, in_sem, sent, red_in, floor_in, hello,
):
    n = part.shape[0]
    chips = n // 2
    me, floor = lax.axis_index("tm"), lax.axis_index("floor")
    chip, core = lax.div(me, 2), lax.rem(me, 2)
    row, col = lax.div(chip, 2), lax.rem(chip, 2)
    sources = [chip, 2 * row + 1 - col, 2 * (1 - row) + col, 2 * (1 - row) + 1 - col]
    other = 1 - core
    pair = 2 * chip + other
    chunks, starts = len(widths), [sum(widths[:j]) for j in range(len(widths))]
    k, depth = x.shape[1], x.shape[2]
    sensors = op.shape[1]
    share_size = sensors // m
    inner = (chip == 1) | (chip == 2)

    def columns(half, j):
        begin, size = (starts[j], widths[j]) if isinstance(j, int) else (j * widths[0], widths[0])
        return pl.ds(pl.multiple_of(half * depth + begin, 128), size)

    def at(j):
        if isinstance(j, int):
            return slice(starts[j], starts[j] + widths[j])
        return pl.ds(pl.multiple_of(j * widths[0], 128), widths[0])

    own = pltpu.make_async_copy(x_hbm.at[0, :, pl.ds(pl.multiple_of(core * depth, 128), depth)], x.at[core], load_sem.at[0])
    staged = pltpu.make_async_copy(x_hbm.at[0], mine, load_sem.at[1])
    weights = pltpu.make_async_copy(
        op_hbm.at[0, :, pl.ds(pl.multiple_of(core * depth, 128), depth)], op.at[core], load_sem.at[2]
    )
    staged.start()
    own.start()

    neighbours = (2 * sources[1], 2 * sources[1] + 1, 2 * sources[2], 2 * sources[2] + 1)

    def to_upper(sem):
        @pl.when(floor < m - 1)
        def _():
            pl.semaphore_signal(sem, inc=1, device_id={"floor": jnp.minimum(floor + 1, m - 1)}, device_id_type=MESH)

    def to_lower(sem):
        @pl.when(floor > 0)
        def _():
            pl.semaphore_signal(sem, inc=1, device_id={"floor": jnp.maximum(floor - 1, 0)}, device_id_type=MESH)

    def in_plane(sem, all_round):
        pl.semaphore_signal(sem, inc=1, device_id={"tm": pair}, device_id_type=MESH)

        @pl.when(all_round)
        def _():
            for target in neighbours:
                pl.semaphore_signal(sem, inc=1, device_id={"tm": target}, device_id_type=MESH)

    def greet(sem):
        in_plane(sem, True)
        to_upper(sem)
        to_lower(sem)

    below, above = jnp.where(floor > 0, 1, 0), jnp.where(floor < m - 1, 1, 0)
    greeted = 5 + below + above
    barrier = pltpu.get_barrier_semaphore()
    in_plane(barrier, chip < chips - 1)
    to_upper(barrier)
    pl.semaphore_wait(barrier, jnp.where(inner, 3, 5) + below)

    @pl.when(chip == chips - 1)
    def _():
        for target in neighbours:
            pl.semaphore_signal(hello.at[2], inc=1, device_id={"tm": target}, device_id_type=MESH)

    to_lower(hello.at[3])

    def need(source, at):
        return source + at < chips

    needs = [need(source, chip) for source in sources]

    def by_x(source, parity, j):
        outer = (source == 0) | (source == chips - 1)
        through_first = jnp.where(source == 1, j == through, j != through)
        return (outer & (parity == j % 2)) | (jnp.logical_not(outer) & through_first)

    def remote(src, dst, out, into, target):
        return pltpu.make_async_remote_copy(
            src_ref=src, dst_ref=dst, send_sem=out, recv_sem=into, device_id={"tm": target}, device_id_type=MESH
        )

    def start(copy):
        copy.start()

    def wait_send(copy):
        copy.wait_send()

    def send_x(j, act):
        @pl.when(needs_at_x | by_x(chip, core, j))
        def _():
            for half in (0, 1):
                act(remote(mine.at[:, columns(half, j)], x.at[2 + core, :, at(j)], sent.at[0], in_sem.at[0, j], 2 * sources[1] + half))

    def send_y(j, act):
        @pl.when(needs_at_y | jnp.logical_not(by_x(chip, core, j)))
        def _():
            for half in (0, 1):
                act(remote(mine.at[:, columns(half, j)], x.at[4 + core, :, at(j)], sent.at[0], in_sem.at[1, j], 2 * sources[2] + half))

    needs_at_x, needs_at_y = need(chip, sources[1]), need(chip, sources[2])

    def send_pair(act):
        there = pl.ds(pl.multiple_of(other * depth, 128), depth)
        act(remote(mine.at[:, there], x.at[core], sent.at[0], pair_in.at[0], pair))

    parts = (slice(0, starts[2]), slice(starts[2], depth))

    def swap(p, act):
        begin, size = parts[p].start, parts[p].stop - parts[p].start
        there = pl.ds(pl.multiple_of(other * depth + begin, 128), size)
        act(remote(op_hbm.at[0, :, there], op.at[core, :, parts[p]], sent.at[0], swap_in.at[p], pair))

    def swapped(p):
        remote(op.at[core, :, parts[p]], op.at[other, :, parts[p]], sent.at[0], swap_in.at[p], pair).wait_recv()

    def taken(source, j, blocks):
        here = x.at[2 * source:2 * source + blocks, :, at(j)]
        remote(here, here, sent.at[0], in_sem.at[source - 1, j], pair).wait_recv()

    def pass_x(j, parity, act):
        act(remote(x.at[2 + parity, :, at(j)], x.at[6 + parity, :, at(j)], sent.at[0], in_sem.at[2, j], 2 * sources[2] + core))

    def pass_y(j, parity, act):
        act(remote(x.at[4 + parity, :, at(j)], x.at[6 + parity, :, at(j)], sent.at[0], in_sem.at[2, j], 2 * sources[1] + core))

    def come(source, j, both, onward):
        count = onward[0].astype(jnp.int32) + onward[1].astype(jnp.int32)
        for blocks in (1, 2):
            @pl.when(jnp.where(both, 2, count) == blocks)
            def _(blocks=blocks):
                taken(source, j, blocks)

    def from_x(j, here, wait, act):
        onward = [by_x(sources[1], parity, j) for parity in (0, 1)]

        @pl.when(here)
        def _():
            if wait:
                come(1, j, needs[1], onward)
            for parity in (0, 1):
                @pl.when(onward[parity])
                def _(parity=parity):
                    pass_x(j, parity, act)

    def from_y(j, here, wait, act):
        onward = [jnp.logical_not(by_x(sources[2], parity, j)) for parity in (0, 1)]

        @pl.when(here)
        def _():
            if wait:
                come(2, j, needs[2], onward)
            for parity in (0, 1):
                @pl.when(onward[parity])
                def _(parity=parity):
                    pass_y(j, parity, act)

    lead = chunks // 2
    staged.wait()
    for j in range(chunks):
        at_once = jnp.logical_not(inner) | (j < lead)

        @pl.when(at_once & needs_at_x)
        def _(j=j):
            send_x(j, start)

        @pl.when(at_once & needs_at_y)
        def _(j=j):
            send_y(j, start)

    across = [*range(lead, chunks), *(j for j in range(lead) if j != through), through]

    def send_only_across(turns):
        for j in turns:
            @pl.when(jnp.logical_not(needs_at_x))
            def _(j=j):
                send_x(j, start)

            @pl.when(jnp.logical_not(needs_at_y))
            def _(j=j):
                send_y(j, start)

    @pl.when(chip == chips - 1)
    def _():
        send_only_across(range(chunks))

    weights.start()
    send_pair(start)
    for p in (0, 1):
        swap(p, start)

    @pl.when(inner)
    def _():
        pl.semaphore_wait(hello.at[2], 2)
        send_only_across(across)

    @pl.when(floor < m - 1)
    def _():
        pl.semaphore_wait(hello.at[3], 1)

    greet(hello.at[0])

    def send_late(j):
        @pl.when(needs_at_x)
        def _():
            send_x(j, start)

        @pl.when(needs_at_y)
        def _():
            send_y(j, start)

    def passing(j):
        from_x(j, jnp.logical_not(needs[1]), True, start)
        from_y(j, jnp.logical_not(needs[2]), True, start)

    @pl.when(inner)
    def _():
        for j in range(chunks):
            passing(j)
            for late in range(lead, chunks):
                if j == min(2 * (late - lead) + 1, chunks - 1):
                    send_late(late)

    @pl.when(chip == chips - 1)
    def _():
        for j in across:
            passing(j)

    pl.semaphore_wait(hello.at[0], greeted)
    greet(hello.at[1])

    def arrive(j):
        from_x(j, needs[1], True, start)
        from_y(j, needs[2], True, start)
    first = chip == 0

    def ready(j):
        if j == 0:
            own.wait()
            weights.wait()
            remote(x.at[other], x.at[other], sent.at[0], pair_in.at[0], pair).wait_recv()
            swapped(0)
        if j == 2:
            swapped(1)

    def multiply(j, pieces):
        rows = jnp.concatenate([x[p, :, at(j)] for p in pieces], axis=0)
        depth_here = rows.shape[-1]
        return lax.dot_general(
            rows.reshape(-1, depth_here), op[:, :, at(j)].reshape(-1, depth_here), (((1,), (1,)), ((), ())),
            preferred_element_type=jnp.float32,
        ).reshape(-1, k, 2 * sensors)

    def compute(j, low, high, begin):
        image = multiply(j, [slice(low, high)])
        if begin:
            acc[low:high] = image
        else:
            acc[low:high] += image

    def compute_ends(j):
        image = multiply(j, [slice(0, 2), slice(6, 8)])
        acc[0:2] += image[0:2]
        acc[6:8] += image[2:4]

    def slot_of(block):
        source = block // 2
        across = jnp.where(col == source % 2, 0, 2) + jnp.where(row == source // 2, 0, 4)
        return across + block % 2

    def place(i):
        return jnp.where(i == m - 1, floor, jnp.where(i < floor, i, i + 1))

    def record(u, j, act):
        act(pltpu.make_async_remote_copy(
            src_ref=sums.at[u, j], dst_ref=part.at[me, j], send_sem=sent.at[1], recv_sem=red_in.at[j],
            device_id={"tm": jnp.minimum(2 * chip + u, n - 1)}, device_id_type=MESH,
        ))

    def records(places, act, add, here=True, low=0, high=m):
        def one(i, _):
            j = place(i)
            mine_at = pl.ds(pl.multiple_of(j * share_size, share_size), share_size)
            there = pl.ds(pl.multiple_of(sensors + j * share_size, share_size), share_size)
            for u in places:
                @pl.when((2 * chip + u < n) & here)
                def _(u=u):
                    if add:
                        sums[u, j] = acc[slot_of(u), :, mine_at] + acc[slot_of(u - 1), :, there]
                    record(u, j, act)

            return 0

        lax.fori_loop(low, high, one, 0)

    def swap_records(act):
        act(remote(sums.at[other], part.at[2 * chip], sent.at[1], pair_in.at[1], pair))

    def own_records():
        for j in range(m):
            mine_at = slice(j * share_size, (j + 1) * share_size)
            there = slice(sensors + j * share_size, sensors + (j + 1) * share_size)
            sums[0, j] = acc[slot_of(0), :, mine_at]
            sums[1, j] = acc[slot_of(1), :, mine_at] + acc[slot_of(0), :, there]
        swap_records(start)

    final = chunks - 1

    @pl.when(jnp.logical_not(inner))
    def _():
        arrive(0)
        arrive(1)
        for j in range(final):
            if j > 1:
                arrive(j)
            ready(j)
            taken(3, j, 2)
            compute(j, 0, n, j == 0)
        ready(final)
        taken(3, final, 2)
        pl.semaphore_wait(hello.at[1], greeted)

        @pl.when(first)
        def _():
            compute_ends(final)
            records((n - 1,), start, True, True, 0, 1)
            own_records()
            arrive(final)
            compute(final, 2, 6, False)
            records((6, 3, 2, 5, 4), start, True, True, 0, 1)
            records((6, 3, 2, 5, 4, n - 1), start, True, True, 1, m)

        @pl.when(jnp.logical_not(first))
        def _():
            compute(final, 0, n, False)
            own_records()

    @pl.when(inner)
    def _():
        for j in range(chunks):
            arrive(j)
            ready(j)
            compute(j, 0, 6, j == 0)
        pl.semaphore_wait(hello.at[1], greeted)
        records((3, 2), start, True, chip == 1)
        own_records()
        for j in across:
            taken(3, j, 2)
            compute(j, 6, 8, j == across[0])
        records((3, 2), start, True, chip == 2)
        records((5, 4), start, True)

    for j in range(chunks):
        send_x(j, wait_send)
        send_y(j, wait_send)
        from_x(j, True, False, wait_send)
        from_y(j, True, False, wait_send)
    send_pair(wait_send)
    for p in (0, 1):
        swap(p, wait_send)

    def to_floor(other, act):
        act(pltpu.make_async_remote_copy(
            src_ref=total.at[other], dst_ref=share.at[floor],
            send_sem=sent.at[2], recv_sem=floor_in.at[0],
            device_id={"floor": other}, device_id_type=MESH,
        ))

    def gather_share(i, _):
        j = place(i)

        for c in range(1, chips):
            @pl.when(chip == c)
            def _(c=c):
                pltpu.make_async_remote_copy(
                    src_ref=sums.at[0:2 * c, j], dst_ref=part.at[0:2 * c, j], send_sem=sent.at[1],
                    recv_sem=red_in.at[j], device_id={"tm": pair}, device_id_type=MESH,
                ).wait_recv()

        def add_part(p, value):
            return value + part[p, j]

        total[j] = lax.fori_loop(0, 2 * chip, add_part, sums[core, j] + part[2 * chip, j])

        @pl.when(j != floor)
        def _():
            to_floor(j, start)

        return 0

    remote(sums.at[0], part.at[2 * chip], sent.at[1], pair_in.at[1], pair).wait_recv()
    lax.fori_loop(0, m, gather_share, 0)
    records(range(n - 1, 1, -1), wait_send, False)
    swap_records(wait_send)
    for step in range(1, m):
        to_floor(lax.rem(floor + step, m), wait_send)
    everyone = pl.ds(0, m - 1)
    pltpu.make_async_remote_copy(
        src_ref=total.at[everyone], dst_ref=share.at[everyone], send_sem=sent.at[2], recv_sem=floor_in.at[0],
        device_id={"floor": lax.rem(floor + 1, m)}, device_id_type=MESH,
    ).wait_recv()
    result = total[floor]
    for step in range(1, m):
        result = result + share[lax.rem(floor + step, m)]
    out_ref[0] = result.astype(out_ref.dtype)


def square_call(n, m, samples, operator):
    _, k, depth = samples.shape
    sensors = operator.shape[1]
    half = depth // 2
    widths = [part * half // 16 for part in (5, 7, 2, 2)]
    chunks = len(widths)
    dma = pltpu.SemaphoreType.DMA
    return pl.pallas_call(
        functools.partial(square, m, widths, 1),
        out_shape=pltpu.VMEM((1, k, sensors // m), jnp.bfloat16),
        in_specs=[pl.BlockSpec(memory_space=pl.ANY)] * 2,
        out_specs=pl.BlockSpec(memory_space=pltpu.VMEM),
        scratch_shapes=[
            pltpu.VMEM((n, k, half), jnp.bfloat16),
            pltpu.VMEM((k, depth), jnp.bfloat16),
            pltpu.VMEM((2, sensors, half), jnp.bfloat16),
            pltpu.VMEM((n, k, 2 * sensors), jnp.float32),
            pltpu.VMEM((n, m, k, sensors // m), jnp.float32),
            pltpu.VMEM((n, m, k, sensors // m), jnp.float32),
            pltpu.VMEM((m, k, sensors // m), jnp.float32),
            pltpu.VMEM((m, k, sensors // m), jnp.float32),
            dma((3,)), dma((2,)), dma((2,)), dma((3, chunks)), dma((3,)), dma((m,)), dma((1,)),
            pltpu.SemaphoreType.REGULAR((4,)),
        ],
        compiler_params=pltpu.CompilerParams(collective_id=0, has_side_effects=True),
    )(samples, operator)


def solution(mesh):
    n, m = mesh.shape["tm"], mesh.shape["floor"]

    def local(samples, operator):
        if grid_of(n // 2) == (2, 2):
            return square_call(n, m, samples, operator)
        _, k, depth = samples.shape
        sensors = operator.shape[1]
        chunks = 4
        width = depth // chunks
        return pl.pallas_call(
            functools.partial(kernel, n, m, chunks),
            out_shape=pltpu.VMEM((1, k, sensors // m), jnp.bfloat16),
            in_specs=[pl.BlockSpec(memory_space=pl.ANY)] * 2,
            out_specs=pl.BlockSpec(memory_space=pltpu.VMEM),
            scratch_shapes=[
                pltpu.VMEM((chunks, n, k, width), jnp.bfloat16),
                pltpu.VMEM((chunks, n, k, width), jnp.bfloat16),
                pltpu.VMEM((chunks, sensors, width), jnp.bfloat16),
                pltpu.VMEM((n, k, sensors), jnp.float32),
                pltpu.VMEM((n, k, sensors), jnp.float32),
                pltpu.VMEM((m, k, sensors // m), jnp.float32),
                pltpu.VMEM((m, k, sensors // m), jnp.float32),
                pltpu.SemaphoreType.DMA((chunks,)),
                pltpu.SemaphoreType.DMA((chunks,)),
                pltpu.SemaphoreType.DMA((chunks, n // 2)),
                pltpu.SemaphoreType.DMA((chunks,)),
                pltpu.SemaphoreType.DMA((chunks, n // 2)),
                pltpu.SemaphoreType.DMA((chunks, n // 2, max(1, max(grid_of(n // 2)) - 1))),
                pltpu.SemaphoreType.DMA((chunks, n)),
                pltpu.SemaphoreType.DMA((n,)),
                pltpu.SemaphoreType.DMA((n,)),
                pltpu.SemaphoreType.DMA((m,)),
                pltpu.SemaphoreType.DMA((m,)),
            ],
            compiler_params=pltpu.CompilerParams(collective_id=0, has_side_effects=True),
        )(samples, operator)

    placed = (P("tm", None, "floor"), P("tm", None, "floor"))
    return jax.shard_map(
        local, mesh=mesh, in_specs=placed, out_specs=P("tm", None, "floor"), check_vma=False
    )
```

```python
import functools

import jax
import jax.numpy as jnp
from jax import lax
from jax.experimental import pallas as pl
from jax.experimental.pallas import tpu as pltpu
from jax.sharding import PartitionSpec as P

MESH = pl.DeviceIdType.MESH
LOOK = 1


def each(low, high, body):
    if high - low <= 4:
        for i in range(low, high):
            body(i)
    else:
        def step(i, carry):
            body(i)
            return carry

        lax.fori_loop(low, high, step, 0)


def grid_of(chips):
    rows = 1
    while rows * rows * 4 <= chips and chips % (rows * 2) == 0:
        rows *= 2
    return rows, chips // rows


def kernel(
    n, m, chunks, x_hbm, op_hbm, out_ref, x, far, op, acc, part, total, share,
    own_sem, op_sem, out_sem, pair_sem, fwd_sem, relay_sem, in_sem,
    red_out, red_in, floor_out, floor_in,
):
    me, floor = lax.axis_index("tm"), lax.axis_index("floor")
    chips = n // 2
    rows, cols = grid_of(chips)
    chip, core = lax.div(me, 2), lax.rem(me, 2)
    row, col = lax.div(chip, cols), lax.rem(chip, cols)
    pair = 2 * chip + 1 - core
    k, width = x.shape[2], x.shape[3]
    sensors = op.shape[1]
    share_size = sensors // m

    def columns(c):
        return pl.ds(c * width, width)

    own = [pltpu.make_async_copy(x_hbm.at[0, :, columns(c)], x.at[c, me], own_sem.at[c]) for c in range(chunks)]
    weights = [pltpu.make_async_copy(op_hbm.at[0, :, columns(c)], op.at[c], op_sem.at[c]) for c in range(chunks)]
    for c in range(chunks):
        own[c].start()
        weights[c].start()

    barrier = pltpu.get_barrier_semaphore()
    for step in range(1, n):
        pl.semaphore_signal(barrier, inc=1, device_id={"tm": lax.rem(me + step, n)}, device_id_type=MESH)
    for step in range(1, m):
        pl.semaphore_signal(barrier, inc=1, device_id={"floor": lax.rem(floor + step, m)}, device_id_type=MESH)
    pl.semaphore_wait(barrier, n + m - 2)

    def need(block, at_chip):
        return 2 * at_chip + block < n

    many = max(rows, cols)

    def straight(source, at):
        return (lax.div(source, cols) == lax.div(at, cols)) | (lax.rem(source, cols) == lax.rem(at, cols))

    def relayed(odd, source, block, at, step):
        turn = lax.rem(core + odd, 2) == 0
        r, q = lax.div(source, cols), lax.rem(source, cols)
        r_at, q_at = lax.div(at, cols), lax.rem(at, cols)
        r_to, q_to = lax.rem(r + step, rows), lax.rem(q + step, cols)
        down = (r_at == r) & (step < rows) & (turn | ((r_to == 0) & (q == 0)))
        along = (q_at == q) & (step < cols) & (jnp.logical_not(turn) | ((q_to == 0) & (r == 0)))
        target = jnp.where(r_at == r, r_to * cols + q_at, r_at * cols + q_to)
        return (at != 0) & (down | along) & need(block, target), 2 * target + core

    def route(odd, source, block, at):
        passes = at < 0
        for step in range(1, many):
            passes = passes | relayed(odd, source, block, at, step)[0]
        return straight(source, at) & (need(block, at) | passes), passes

    def make_plan(step, odd):
        other = lax.rem(chip + step, chips)
        block = 2 * other + core
        wanted, _ = route(odd, chip, me, other)
        _, passes = route(odd, other, block, chip)
        near = straight(other, chip)
        here = need(block, chip) & near, need(block, chip) & jnp.logical_not(near)
        alone = here[0] & jnp.logical_not(passes)
        onward = [relayed(odd, other, block, chip, s) for s in range(1, many)]
        return other, block, wanted, passes, here, alone, onward

    plans = {}
    if chips <= 5:
        plans = {(step, odd): make_plan(step, odd) for step in range(1, chips) for odd in (0, 1)}

    def plan(step, c):
        return plans[step, c % 2] if plans else make_plan(step, c % 2)

    others = [2 * lax.rem(chip + step, chips) + 1 - core for step in range(chips)] if plans else None
    def other_here(block):
        near = straight(lax.div(block, 2), chip)
        return need(block, chip) & near, need(block, chip) & jnp.logical_not(near)

    others_here = [other_here(block) for block in others] if plans else None
    self_here = need(me, chip)

    busy = need(2 * row * cols, chip) | need(2 * col, chip)

    def send(c, block, target, sem, source=None, into=None):
        return pltpu.make_async_remote_copy(
            src_ref=x.at[c, block] if source is None else source,
            dst_ref=(x if into is None else into).at[c, block],
            send_sem=sem, recv_sem=in_sem.at[c, block], device_id={"tm": target}, device_id_type=MESH,
        )

    def mine(c):
        return x_hbm.at[0, :, columns(c)]

    def sends(c, act):
        def one(step):
            _, block, wanted, *_ = plan(step, c)

            @pl.when(wanted)
            def _():
                act(send(c, me, block, out_sem.at[c, step], mine(c)))

        each(1, chips, one)

        @pl.when(self_here)
        def _():
            act(send(c, me, pair, pair_sem.at[c], mine(c)))

    def relays(c, act, wait):
        def one(step):
            source, block, _, passes, _, _, onward = plan(step, c)

            @pl.when(passes)
            def _():
                if wait:
                    send(c, block, pair, fwd_sem.at[c, source]).wait_recv()
                for s, (wanted, target) in enumerate(onward):
                    @pl.when(wanted)
                    def _(s=s, target=target):
                        act(send(c, block, target, relay_sem.at[c, source, s], None, far))

        each(1, chips, one)

    def forwards(c, act, wait):
        def one(step):
            source, block, _, _, here, alone, _ = plan(step, c)
            if wait:
                @pl.when(alone)
                def _():
                    send(c, block, pair, fwd_sem.at[c, source]).wait_recv()

            @pl.when(here[0])
            def _():
                act(send(c, block, pair, fwd_sem.at[c, source]))

        each(1, chips, one)

    def far_forwards(c, act, wait):
        def one(step):
            source, block, _, _, here, _, _ = plan(step, c)

            @pl.when(here[1])
            def _():
                copy = send(c, block, pair, fwd_sem.at[c, source], far.at[c, block], far)
                if wait:
                    copy.wait_recv()
                act(copy)

        each(1, chips, one)

    def take(c, part_of):
        def one(step):
            block = others[step] if plans else 2 * lax.rem(chip + step, chips) + 1 - core
            here = (others_here[step] if plans else other_here(block))[part_of]

            @pl.when(here)
            def _():
                send(c, block, pair, pair_sem.at[c], None, far if part_of else None).wait_recv()

        each(0, chips, one)

    def start(copy):
        copy.start()

    def wait_send(copy):
        copy.wait_send()


    tile = min(n, max(1, 128 // k))

    def image_of(block_rows, c):
        return lax.dot_general(
            block_rows.reshape(-1, width), op[c], (((1,), (1,)), ((), ())), preferred_element_type=jnp.float32
        ).reshape(-1, k, sensors)

    for c in range(chunks):
        sends(c, start)
    for c in range(min(LOOK, chunks)):
        relays(c, start, True)
    forwards(0, start, True)
    for c in range(chunks):
        if c + LOOK < chunks:
            relays(c + LOOK, start, True)
        if c + 1 < chunks:
            forwards(c + 1, start, True)
        take(c, 0)
        own[c].wait()
        weights[c].wait()

        @pl.when(busy)
        def _(c=c):
            for r in range(n // tile):
                image = image_of(x[c, r * tile:(r + 1) * tile], c)
                if c == 0:
                    acc[r * tile:(r + 1) * tile] = image
                else:
                    acc[r * tile:(r + 1) * tile] += image

    def lag_part(step):
        return pltpu.make_async_remote_copy(
            src_ref=acc.at[step], dst_ref=part.at[me],
            send_sem=red_out.at[step], recv_sem=red_in.at[me],
            device_id={"tm": lax.rem(me + step, n)}, device_id_type=MESH,
        )

    def lag_parts(near, act):
        for step in range(n - 1, 0, -1):
            @pl.when((me + step < n) & (straight(step // 2, chip) == near))
            def _(step=step):
                act(lag_part(step))

    lag_parts(True, start)

    far_forwards(0, start, True)
    for c in range(chunks):
        if c + 1 < chunks:
            far_forwards(c + 1, start, True)
        take(c, 1)

        def far_images(step, c=c):
            r = lax.rem(row + 1 + lax.div(step, max(1, cols - 1)), rows)
            q = lax.rem(col + 1 + lax.rem(step, max(1, cols - 1)), cols)
            source = r * cols + q

            @pl.when(need(2 * source, chip))
            def _():
                image = image_of(far[c, pl.ds(2 * source, 2)], c)
                if c == 0:
                    acc[pl.ds(2 * source, 2)] = image
                else:
                    acc[pl.ds(2 * source, 2)] += image

        each(0, (rows - 1) * (cols - 1), far_images)

    lag_parts(False, start)

    for c in range(chunks):
        sends(c, wait_send)
        relays(c, wait_send, False)
        forwards(c, wait_send, False)
        far_forwards(c, wait_send, False)

    def add_lag(lag, value):
        pltpu.make_async_remote_copy(
            src_ref=acc.at[0], dst_ref=part.at[lag],
            send_sem=red_out.at[0], recv_sem=red_in.at[lag],
            device_id={"tm": pair}, device_id_type=MESH,
        ).wait_recv()
        return value + part[lag]

    value = lax.fori_loop(0, me, add_lag, acc[0])
    for j in range(m):
        total[j] = value[:, j * share_size:(j + 1) * share_size]

    def to_floor(step):
        other = lax.rem(floor + step, m)
        return pltpu.make_async_remote_copy(
            src_ref=total.at[other], dst_ref=share.at[floor],
            send_sem=floor_out.at[step], recv_sem=floor_in.at[floor],
            device_id={"floor": other}, device_id_type=MESH,
        )

    for step in range(m - 1, 0, -1):
        to_floor(step).start()
    result = total[floor]
    for step in range(1, m):
        source = lax.rem(floor + step, m)
        pltpu.make_async_remote_copy(
            src_ref=total.at[source], dst_ref=share.at[source],
            send_sem=floor_out.at[step], recv_sem=floor_in.at[source],
            device_id={"floor": source}, device_id_type=MESH,
        ).wait_recv()
        result = result + share[source]
    out_ref[0] = result.astype(out_ref.dtype)

    lag_parts(True, wait_send)
    lag_parts(False, wait_send)
    for step in range(1, m):
        to_floor(step).wait_send()


def square(
    m, widths, through, x_hbm, op_hbm, out_ref, x, mine, op, acc, sums, part, total, share,
    load_sem, swap_in, pair_in, in_sem, sent, red_in, floor_in, hello,
):
    n = part.shape[0]
    chips = n // 2
    me, floor = lax.axis_index("tm"), lax.axis_index("floor")
    chip, core = lax.div(me, 2), lax.rem(me, 2)
    row, col = lax.div(chip, 2), lax.rem(chip, 2)
    sources = [chip, 2 * row + 1 - col, 2 * (1 - row) + col, 2 * (1 - row) + 1 - col]
    other = 1 - core
    pair = 2 * chip + other
    chunks, starts = len(widths), [sum(widths[:j]) for j in range(len(widths))]
    k, depth = x.shape[1], x.shape[2]
    sensors = op.shape[1]
    share_size = sensors // m
    inner = (chip == 1) | (chip == 2)

    def columns(half, j):
        begin, size = (starts[j], widths[j]) if isinstance(j, int) else (j * widths[0], widths[0])
        return pl.ds(pl.multiple_of(half * depth + begin, 128), size)

    def at(j):
        if isinstance(j, int):
            return slice(starts[j], starts[j] + widths[j])
        return pl.ds(pl.multiple_of(j * widths[0], 128), widths[0])

    own = pltpu.make_async_copy(x_hbm.at[0, :, pl.ds(pl.multiple_of(core * depth, 128), depth)], x.at[core], load_sem.at[0])
    staged = pltpu.make_async_copy(x_hbm.at[0], mine, load_sem.at[1])
    weights = pltpu.make_async_copy(
        op_hbm.at[0, :, pl.ds(pl.multiple_of(core * depth, 128), depth)], op.at[core], load_sem.at[2]
    )
    staged.start()
    own.start()

    neighbours = (2 * sources[1], 2 * sources[1] + 1, 2 * sources[2], 2 * sources[2] + 1)

    def to_upper(sem):
        @pl.when(floor < m - 1)
        def _():
            pl.semaphore_signal(sem, inc=1, device_id={"floor": jnp.minimum(floor + 1, m - 1)}, device_id_type=MESH)

    def to_lower(sem):
        @pl.when(floor > 0)
        def _():
            pl.semaphore_signal(sem, inc=1, device_id={"floor": jnp.maximum(floor - 1, 0)}, device_id_type=MESH)

    def in_plane(sem, all_round):
        pl.semaphore_signal(sem, inc=1, device_id={"tm": pair}, device_id_type=MESH)

        @pl.when(all_round)
        def _():
            for target in neighbours:
                pl.semaphore_signal(sem, inc=1, device_id={"tm": target}, device_id_type=MESH)

    def greet(sem):
        in_plane(sem, True)
        to_upper(sem)
        to_lower(sem)

    below, above = jnp.where(floor > 0, 1, 0), jnp.where(floor < m - 1, 1, 0)
    greeted = 5 + below + above
    barrier = pltpu.get_barrier_semaphore()
    in_plane(barrier, chip < chips - 1)
    to_upper(barrier)
    pl.semaphore_wait(barrier, jnp.where(inner, 3, 5) + below)

    @pl.when(chip == chips - 1)
    def _():
        for target in neighbours:
            pl.semaphore_signal(hello.at[2], inc=1, device_id={"tm": target}, device_id_type=MESH)

    to_lower(hello.at[3])

    def need(source, at):
        return source + at < chips

    needs = [need(source, chip) for source in sources]

    def by_x(source, parity, j):
        outer = (source == 0) | (source == chips - 1)
        through_first = jnp.where(source == 1, j == through, j != through)
        return (outer & (parity == j % 2)) | (jnp.logical_not(outer) & through_first)

    def remote(src, dst, out, into, target):
        return pltpu.make_async_remote_copy(
            src_ref=src, dst_ref=dst, send_sem=out, recv_sem=into, device_id={"tm": target}, device_id_type=MESH
        )

    def start(copy):
        copy.start()

    def wait_send(copy):
        copy.wait_send()

    def send_x(j, act):
        @pl.when(needs_at_x | by_x(chip, core, j))
        def _():
            for half in (0, 1):
                act(remote(mine.at[:, columns(half, j)], x.at[2 + core, :, at(j)], sent.at[0], in_sem.at[0, j], 2 * sources[1] + half))

    def send_y(j, act):
        @pl.when(needs_at_y | jnp.logical_not(by_x(chip, core, j)))
        def _():
            for half in (0, 1):
                act(remote(mine.at[:, columns(half, j)], x.at[4 + core, :, at(j)], sent.at[0], in_sem.at[1, j], 2 * sources[2] + half))

    needs_at_x, needs_at_y = need(chip, sources[1]), need(chip, sources[2])

    def send_pair(act):
        there = pl.ds(pl.multiple_of(other * depth, 128), depth)
        act(remote(mine.at[:, there], x.at[core], sent.at[0], pair_in.at[0], pair))

    parts = (slice(0, starts[2]), slice(starts[2], depth))

    def swap(p, act):
        begin, size = parts[p].start, parts[p].stop - parts[p].start
        there = pl.ds(pl.multiple_of(other * depth + begin, 128), size)
        act(remote(op_hbm.at[0, :, there], op.at[core, :, parts[p]], sent.at[0], swap_in.at[p], pair))

    def swapped(p):
        remote(op.at[core, :, parts[p]], op.at[other, :, parts[p]], sent.at[0], swap_in.at[p], pair).wait_recv()

    def taken(source, j, blocks):
        here = x.at[2 * source:2 * source + blocks, :, at(j)]
        remote(here, here, sent.at[0], in_sem.at[source - 1, j], pair).wait_recv()

    def pass_x(j, parity, act):
        act(remote(x.at[2 + parity, :, at(j)], x.at[6 + parity, :, at(j)], sent.at[0], in_sem.at[2, j], 2 * sources[2] + core))

    def pass_y(j, parity, act):
        act(remote(x.at[4 + parity, :, at(j)], x.at[6 + parity, :, at(j)], sent.at[0], in_sem.at[2, j], 2 * sources[1] + core))

    def come(source, j, both, onward):
        count = onward[0].astype(jnp.int32) + onward[1].astype(jnp.int32)
        for blocks in (1, 2):
            @pl.when(jnp.where(both, 2, count) == blocks)
            def _(blocks=blocks):
                taken(source, j, blocks)

    def from_x(j, here, wait, act):
        onward = [by_x(sources[1], parity, j) for parity in (0, 1)]

        @pl.when(here)
        def _():
            if wait:
                come(1, j, needs[1], onward)
            for parity in (0, 1):
                @pl.when(onward[parity])
                def _(parity=parity):
                    pass_x(j, parity, act)

    def from_y(j, here, wait, act):
        onward = [jnp.logical_not(by_x(sources[2], parity, j)) for parity in (0, 1)]

        @pl.when(here)
        def _():
            if wait:
                come(2, j, needs[2], onward)
            for parity in (0, 1):
                @pl.when(onward[parity])
                def _(parity=parity):
                    pass_y(j, parity, act)

    lead = chunks // 2
    staged.wait()
    for j in range(chunks):
        at_once = jnp.logical_not(inner) | (j < lead)

        @pl.when(at_once & needs_at_x)
        def _(j=j):
            send_x(j, start)

        @pl.when(at_once & needs_at_y)
        def _(j=j):
            send_y(j, start)

    across = [*range(lead, chunks), *(j for j in range(lead) if j != through), through]

    def send_only_across(turns):
        for j in turns:
            @pl.when(jnp.logical_not(needs_at_x))
            def _(j=j):
                send_x(j, start)

            @pl.when(jnp.logical_not(needs_at_y))
            def _(j=j):
                send_y(j, start)

    @pl.when(chip == chips - 1)
    def _():
        send_only_across(range(chunks))

    weights.start()
    send_pair(start)
    for p in (0, 1):
        swap(p, start)

    @pl.when(inner)
    def _():
        pl.semaphore_wait(hello.at[2], 2)
        send_only_across(across)

    @pl.when(floor < m - 1)
    def _():
        pl.semaphore_wait(hello.at[3], 1)

    greet(hello.at[0])

    def send_late(j):
        @pl.when(needs_at_x)
        def _():
            send_x(j, start)

        @pl.when(needs_at_y)
        def _():
            send_y(j, start)

    def passing(j):
        from_x(j, jnp.logical_not(needs[1]), True, start)
        from_y(j, jnp.logical_not(needs[2]), True, start)

    @pl.when(inner)
    def _():
        for j in range(chunks):
            passing(j)
            for late in range(lead, chunks):
                if j == min(2 * (late - lead) + 1, chunks - 1):
                    send_late(late)

    @pl.when(chip == chips - 1)
    def _():
        for j in across:
            passing(j)

    pl.semaphore_wait(hello.at[0], greeted)
    greet(hello.at[1])

    def arrive(j):
        from_x(j, needs[1], True, start)
        from_y(j, needs[2], True, start)
    first = chip == 0

    def ready(j):
        if j == 0:
            own.wait()
            weights.wait()
            remote(x.at[other], x.at[other], sent.at[0], pair_in.at[0], pair).wait_recv()
            swapped(0)
        if j == 2:
            swapped(1)

    def multiply(j, pieces):
        rows = jnp.concatenate([x[p, :, at(j)] for p in pieces], axis=0)
        depth_here = rows.shape[-1]
        return lax.dot_general(
            rows.reshape(-1, depth_here), op[:, :, at(j)].reshape(-1, depth_here), (((1,), (1,)), ((), ())),
            preferred_element_type=jnp.float32,
        ).reshape(-1, k, 2 * sensors)

    def compute(j, low, high, begin):
        image = multiply(j, [slice(low, high)])
        if begin:
            acc[low:high] = image
        else:
            acc[low:high] += image

    def compute_ends(j):
        image = multiply(j, [slice(0, 2), slice(6, 8)])
        acc[0:2] += image[0:2]
        acc[6:8] += image[2:4]

    def slot_of(block):
        source = block // 2
        across = jnp.where(col == source % 2, 0, 2) + jnp.where(row == source // 2, 0, 4)
        return across + block % 2

    def place(i):
        return jnp.where(i == m - 1, floor, jnp.where(i < floor, i, i + 1))

    def record(u, j, act):
        act(pltpu.make_async_remote_copy(
            src_ref=sums.at[u, j], dst_ref=part.at[me, j], send_sem=sent.at[0], recv_sem=red_in.at[j],
            device_id={"tm": jnp.minimum(2 * chip + u, n - 1)}, device_id_type=MESH,
        ))

    def records(places, act, add, here=True, low=0, high=m):
        def one(i, _):
            j = place(i)
            mine_at = pl.ds(pl.multiple_of(j * share_size, share_size), share_size)
            there = pl.ds(pl.multiple_of(sensors + j * share_size, share_size), share_size)
            for u in places:
                @pl.when((2 * chip + u < n) & here)
                def _(u=u):
                    if add:
                        sums[u, j] = acc[slot_of(u), :, mine_at] + acc[slot_of(u - 1), :, there]
                    record(u, j, act)

            return 0

        lax.fori_loop(low, high, one, 0)

    def swap_records(act):
        act(remote(sums.at[other], part.at[2 * chip], sent.at[0], pair_in.at[1], pair))

    def own_records():
        for j in range(m):
            mine_at = slice(j * share_size, (j + 1) * share_size)
            there = slice(sensors + j * share_size, sensors + (j + 1) * share_size)
            sums[0, j] = acc[slot_of(0), :, mine_at]
            sums[1, j] = acc[slot_of(1), :, mine_at] + acc[slot_of(0), :, there]
        swap_records(start)

    final = chunks - 1

    @pl.when(jnp.logical_not(inner))
    def _():
        arrive(0)
        arrive(1)
        for j in range(final):
            if j > 1:
                arrive(j)
            ready(j)
            taken(3, j, 2)
            compute(j, 0, n, j == 0)
        ready(final)
        taken(3, final, 2)
        pl.semaphore_wait(hello.at[1], greeted)

        @pl.when(first)
        def _():
            compute_ends(final)
            records((n - 1,), start, True, True, 0, 1)
            own_records()
            arrive(final)
            compute(final, 2, 6, False)
            records((6, 3, 2, 5, 4), start, True, True, 0, 1)
            records((6, 3, 2, 5, 4, n - 1), start, True, True, 1, m)

        @pl.when(jnp.logical_not(first))
        def _():
            compute(final, 0, n, False)
            own_records()

    @pl.when(inner)
    def _():
        for j in range(chunks):
            arrive(j)
            ready(j)
            compute(j, 0, 6, j == 0)
        pl.semaphore_wait(hello.at[1], greeted)
        records((3, 2), start, True, chip == 1)
        own_records()
        for j in across:
            taken(3, j, 2)
            compute(j, 6, 8, j == across[0])
        records((3, 2), start, True, chip == 2)
        records((5, 4), start, True)

    def to_floor(other, act):
        act(pltpu.make_async_remote_copy(
            src_ref=total.at[other], dst_ref=share.at[floor],
            send_sem=sent.at[0], recv_sem=floor_in.at[0],
            device_id={"floor": other}, device_id_type=MESH,
        ))

    def gather_share(i, _):
        j = place(i)

        for c in range(1, chips):
            @pl.when(chip == c)
            def _(c=c):
                pltpu.make_async_remote_copy(
                    src_ref=sums.at[0:2 * c, j], dst_ref=part.at[0:2 * c, j], send_sem=sent.at[0],
                    recv_sem=red_in.at[j], device_id={"tm": pair}, device_id_type=MESH,
                ).wait_recv()

        def add_part(p, value):
            return value + part[p, j]

        total[j] = lax.fori_loop(0, 2 * chip, add_part, sums[core, j] + part[2 * chip, j])

        @pl.when(j != floor)
        def _():
            to_floor(j, start)

        return 0

    remote(sums.at[0], part.at[2 * chip], sent.at[0], pair_in.at[1], pair).wait_recv()
    lax.fori_loop(0, m, gather_share, 0)
    for j in range(chunks):
        send_x(j, wait_send)
        send_y(j, wait_send)
        from_x(j, True, False, wait_send)
        from_y(j, True, False, wait_send)
    send_pair(wait_send)
    for p in (0, 1):
        swap(p, wait_send)
    records(range(n - 1, 1, -1), wait_send, False)
    swap_records(wait_send)
    for step in range(1, m):
        to_floor(lax.rem(floor + step, m), wait_send)
    everyone = pl.ds(0, m - 1)
    pltpu.make_async_remote_copy(
        src_ref=total.at[everyone], dst_ref=share.at[everyone], send_sem=sent.at[0], recv_sem=floor_in.at[0],
        device_id={"floor": lax.rem(floor + 1, m)}, device_id_type=MESH,
    ).wait_recv()
    result = total[floor]
    for step in range(1, m):
        result = result + share[lax.rem(floor + step, m)]
    out_ref[0] = result.astype(out_ref.dtype)


def square_call(n, m, samples, operator):
    _, k, depth = samples.shape
    sensors = operator.shape[1]
    half = depth // 2
    widths = [part * half // 16 for part in (5, 7, 2, 2)]
    chunks = len(widths)
    dma = pltpu.SemaphoreType.DMA
    return pl.pallas_call(
        functools.partial(square, m, widths, 1),
        out_shape=pltpu.VMEM((1, k, sensors // m), jnp.bfloat16),
        in_specs=[pl.BlockSpec(memory_space=pl.ANY)] * 2,
        out_specs=pl.BlockSpec(memory_space=pltpu.VMEM),
        scratch_shapes=[
            pltpu.VMEM((n, k, half), jnp.bfloat16),
            pltpu.VMEM((k, depth), jnp.bfloat16),
            pltpu.VMEM((2, sensors, half), jnp.bfloat16),
            pltpu.VMEM((n, k, 2 * sensors), jnp.float32),
            pltpu.VMEM((n, m, k, sensors // m), jnp.float32),
            pltpu.VMEM((n, m, k, sensors // m), jnp.float32),
            pltpu.VMEM((m, k, sensors // m), jnp.float32),
            pltpu.VMEM((m, k, sensors // m), jnp.float32),
            dma((3,)), dma((2,)), dma((2,)), dma((3, chunks)), dma((1,)), dma((m,)), dma((1,)),
            pltpu.SemaphoreType.REGULAR((4,)),
        ],
        compiler_params=pltpu.CompilerParams(collective_id=0, has_side_effects=True),
    )(samples, operator)


def solution(mesh):
    n, m = mesh.shape["tm"], mesh.shape["floor"]

    def local(samples, operator):
        if grid_of(n // 2) == (2, 2):
            return square_call(n, m, samples, operator)
        _, k, depth = samples.shape
        sensors = operator.shape[1]
        chunks = 4
        width = depth // chunks
        return pl.pallas_call(
            functools.partial(kernel, n, m, chunks),
            out_shape=pltpu.VMEM((1, k, sensors // m), jnp.bfloat16),
            in_specs=[pl.BlockSpec(memory_space=pl.ANY)] * 2,
            out_specs=pl.BlockSpec(memory_space=pltpu.VMEM),
            scratch_shapes=[
                pltpu.VMEM((chunks, n, k, width), jnp.bfloat16),
                pltpu.VMEM((chunks, n, k, width), jnp.bfloat16),
                pltpu.VMEM((chunks, sensors, width), jnp.bfloat16),
                pltpu.VMEM((n, k, sensors), jnp.float32),
                pltpu.VMEM((n, k, sensors), jnp.float32),
                pltpu.VMEM((m, k, sensors // m), jnp.float32),
                pltpu.VMEM((m, k, sensors // m), jnp.float32),
                pltpu.SemaphoreType.DMA((chunks,)),
                pltpu.SemaphoreType.DMA((chunks,)),
                pltpu.SemaphoreType.DMA((chunks, n // 2)),
                pltpu.SemaphoreType.DMA((chunks,)),
                pltpu.SemaphoreType.DMA((chunks, n // 2)),
                pltpu.SemaphoreType.DMA((chunks, n // 2, max(1, max(grid_of(n // 2)) - 1))),
                pltpu.SemaphoreType.DMA((chunks, n)),
                pltpu.SemaphoreType.DMA((n,)),
                pltpu.SemaphoreType.DMA((n,)),
                pltpu.SemaphoreType.DMA((m,)),
                pltpu.SemaphoreType.DMA((m,)),
            ],
            compiler_params=pltpu.CompilerParams(collective_id=0, has_side_effects=True),
        )(samples, operator)

    placed = (P("tm", None, "floor"), P("tm", None, "floor"))
    return jax.shard_map(
        local, mesh=mesh, in_specs=placed, out_specs=P("tm", None, "floor"), check_vma=False
    )
```
